32 devices in a mesh: samp: 8 (over y, x, core), sx: 2 (over z_hi), sy: 2 (over z_lo).
Axes of the slice: x: 2, y: 2, z: 4 (z_hi: 2, z_lo: 2; z = z_hi * 2 + z_lo), core: 2. Of those that a mesh axis runs over, the one named last changes fastest.
Arguments:
- volume: bfloat16 [8, 32, 4, 16, 128], P('samp', None, 'sx', 'sy'), may hold values from -6 to 6
- kernel: bfloat16 [64, 32, 3, 3, 3], replicated, may hold values from -0.21875 to 0.21875
- bias: float32 [64], replicated, may hold values from -4 to 4
- upstream: bfloat16 [8, 64, 4, 16, 128], P('samp', None, 'sx', 'sy'), may hold values from -6 to 6
Outputs:
- activated: bfloat16 [8, 64, 4, 16, 128], P('samp', None, 'sx', 'sy')
- input_grad: bfloat16 [8, 32, 4, 16, 128], P('samp', None, 'sx', 'sy')
- filter_grad: float32 [64, 32, 3, 3, 3], replicated
- bias_grad: float32 [64], replicated
The draws below stay inside these ranges and needn't reach their ends.
All inputs are finite; a program needn't handle non-finite values.
Results may differ from the reference program's by a relative error of at most 0.0065.
Values may be sent and summed in bfloat16 or wider, within the bound.
A program may use at most 64 MiB of HBM per device.

```python
import jax
import jax.numpy as jnp
from jax import lax

CIN = 32
COUT = 64
Z = 128
B = 8
X = 4
Y = 16


def levels(stream_key, dims, pieces, least, largest):
    gain = 1.0
    for position, shards_of in pieces:
        steps = jax.random.uniform(jax.random.fold_in(jax.random.fold_in(stream_key, 6), position), (shards_of,), jnp.float32, least / len(pieces), largest / len(pieces))
        gain = gain * jnp.repeat(jnp.exp(steps), dims[position] // shards_of).reshape((-1,) + (1,) * (len(dims) - 1 - position))
    return gain


def noise(own_key, dims, spread, bound, shards=(), kind=jnp.bfloat16):
    values = spread * jax.random.normal(own_key, dims, jnp.float32)
    if shards:
        values = values * levels(own_key, dims, shards, -0.22, 0.18)
    return jnp.clip(values, -bound, bound).astype(kind)


def setup_inputs(seed: int = 0) -> dict:
    keys = jax.random.split(jax.random.key(seed), 5)
    return {
        "volume": noise(keys[0], (B, CIN, X, Y, Z), 1.0, 6.0, ((0, 8), (2, 2), (3, 2))),
        "kernel": noise(keys[1], (COUT, CIN, 3, 3, 3), (27 * CIN) ** -0.5, 0.21875),
        "bias": noise(keys[2], (COUT,), 1.0, 4.0, (), jnp.float32),
        "upstream": noise(keys[3], (B, COUT, X, Y, Z), 1.0, 6.0, ((0, 8), (2, 2), (3, 2))),
    }


def conv_forward(padded, kernel, rows, cols, depth):
    total = None
    for a in range(3):
        for b in range(3):
            for c in range(3):
                piece = padded[:, a:a + rows, b:b + cols, c:c + depth].reshape(padded.shape[0], -1)
                term = jnp.dot(kernel[:, :, a, b, c], piece, preferred_element_type=jnp.float32)
                total = term if total is None else total + term
    return total.reshape(kernel.shape[0], rows, cols, depth)

def conv_backward(padded, kernel, rows, cols, depth):
    total = None
    for a in range(3):
        for b in range(3):
            for c in range(3):
                piece = padded[:, 2 - a:2 - a + rows, 2 - b:2 - b + cols, 2 - c:2 - c + depth].reshape(padded.shape[0], -1)
                term = jnp.dot(kernel[:, :, a, b, c].T, piece, preferred_element_type=jnp.float32)
                total = term if total is None else total + term
    return total.reshape(kernel.shape[1], rows, cols, depth)

def filter_terms(padded, delta, rows, cols, depth):
    flat_delta = delta.reshape(delta.shape[0], -1)
    terms = []
    for a in range(3):
        for b in range(3):
            for c in range(3):
                piece = padded[:, a:a + rows, b:b + cols, c:c + depth].reshape(padded.shape[0], -1)
                terms.append(jnp.dot(flat_delta, piece.T, preferred_element_type=jnp.float32))
    return jnp.stack(terms, axis=-1).reshape(delta.shape[0], padded.shape[0], 3, 3, 3)

def one_sample(items, kernel, bias):
    sample, grad_out = items
    rows, cols, depth = (sample.shape[1], sample.shape[2], sample.shape[3])
    padded = jnp.pad(sample, ((0, 0), (1, 1), (1, 1), (1, 1)))
    pre = conv_forward(padded, kernel, rows, cols, depth) + bias[:, None, None, None]
    activated = (0.3 * pre + 0.7 * jax.nn.softplus(pre)).astype(jnp.bfloat16)
    delta = (grad_out.astype(jnp.float32) * (0.3 + 0.7 * jax.nn.sigmoid(pre))).astype(jnp.bfloat16)
    delta_pad = jnp.pad(delta, ((0, 0), (1, 1), (1, 1), (1, 1)))
    input_grad = conv_backward(delta_pad, kernel, rows, cols, depth).astype(jnp.bfloat16)
    wgrad = filter_terms(padded, delta, rows, cols, depth)
    bgrad = lax.optimization_barrier(jnp.sum(delta.astype(jnp.float32), axis=(1, 2, 3)))
    return (activated, input_grad, wgrad, bgrad)

def reference(volume, kernel, bias, upstream):
    activated, input_grad, wgrad, bgrad = lax.map(lambda items: one_sample(items, kernel, bias), (volume, upstream))
    norm = 1.0 / jnp.sqrt(jnp.float32(volume.shape[0] * volume.shape[2] * volume.shape[3] * volume.shape[4]))
    return (activated, input_grad, lax.optimization_barrier(jnp.sum(wgrad, axis=0)) * norm, lax.optimization_barrier(jnp.sum(bgrad, axis=0)) * norm)
```

```python
import functools
import math

import jax
import jax.numpy as jnp
from jax import lax
from jax.experimental import pallas as pl
from jax.experimental.pallas import tpu as pltpu
from jax.sharding import PartitionSpec as P

MESH = pl.DeviceIdType.MESH
F32 = jnp.float32
BF16 = jnp.bfloat16
DIRS = tuple((dx, dy) for dx in (-1, 0, 1) for dy in (-1, 0, 1) if dx or dy)


def each(count, fn):
    if count <= 8:
        for k in range(1, count):
            fn(k)
    else:
        lax.fori_loop(1, count, lambda k, c: (fn(k), c)[1], 0)


def span(step, size):
    if step > 0:
        return pl.ds(size, 1), pl.ds(0, 1), size
    if step < 0:
        return pl.ds(1, 1), pl.ds(size + 1, 1), 1
    return pl.ds(1, size), pl.ds(1, size), 1


def kernel(
    dims, sizes, chunk, norm,
    vol_ref, w_ref, bias_ref, up_ref,
    act_ref, ig_ref, wg_ref, bg_ref,
    vol_s, up_s, act_s, ig_s, pad, dpad, col, dcol, sd, wt, wb, stage, part, r1, r2, gat,
    hs1, hr1, hs2, hr2, s1, v1, s2, v2, s3, v3,
):
    rows, cols, cin, cout, depth = dims
    n_samp, n_sx, n_sy = sizes
    owners, crows = chunk
    cells = rows * cols
    group = n_sx * n_sy
    me = lax.axis_index("samp")
    ix, iy = lax.axis_index("sx"), lax.axis_index("sy")
    gid = ix * n_sy + iy

    barrier = pltpu.get_barrier_semaphore()

    def greet_samp(k):
        pl.semaphore_signal(barrier, inc=1, device_id={"samp": lax.rem(me + k, n_samp)}, device_id_type=MESH)

    def group_id(k):
        g = lax.rem(gid + k, group)
        return g, {"sx": lax.div(g, n_sy), "sy": lax.rem(g, n_sy)}

    def greet_group(k):
        pl.semaphore_signal(barrier, inc=1, device_id=group_id(k)[1], device_id_type=MESH)

    each(n_samp, greet_samp)
    each(group, greet_group)

    def has(dx, dy):
        ok = None
        for i, step, size in ((ix, dx, n_sx), (iy, dy, n_sy)):
            if step:
                one = (i + 1 < size) if step > 0 else (i > 0)
                ok = one if ok is None else jnp.logical_and(ok, one)
        return ok

    def halo(buf, ss, rs, d):
        dx, dy = DIRS[d]
        sx, tx, _ = span(dx, rows)
        sy, ty, _ = span(dy, cols)
        return pltpu.make_async_remote_copy(
            src_ref=buf.at[sx, sy], dst_ref=buf.at[tx, ty],
            send_sem=ss.at[d], recv_sem=rs.at[d],
            device_id={"sx": ix + dx, "sy": iy + dy}, device_id_type=MESH,
        )

    live = [d for d, (dx, dy) in enumerate(DIRS) if not ((dx and n_sx == 1) or (dy and n_sy == 1))]

    def halo_zero(buf):
        for d, (dx, dy) in enumerate(DIRS):
            _, tx, _ = span(dx, rows)
            _, ty, _ = span(dy, cols)

            def clear():
                v = buf[tx, ty]
                buf[tx, ty] = jnp.zeros_like(v)

            if d in live:
                pl.when(jnp.logical_not(has(-dx, -dy)))(clear)
            else:
                clear()

    def halo_send(buf, ss, rs):
        for d in live:
            pl.when(has(*DIRS[d]))(lambda: halo(buf, ss, rs, d).start())

    def halo_recv(buf, ss, rs):
        for d in live:
            dx, dy = DIRS[d]
            pl.when(has(-dx, -dy))(lambda: halo(buf, ss, rs, d).wait_recv())

    def halo_sent(buf, ss, rs):
        for d in live:
            pl.when(has(*DIRS[d]))(lambda: halo(buf, ss, rs, d).wait_send())

    vol_s[...] = vol_ref[...].astype(F32)
    for x in range(rows):
        for y in range(cols):
            pad[1 + x, 1 + y] = vol_s[pl.ds(x * cols + y, cin, stride=cells), :].astype(BF16)
    pl.semaphore_wait(barrier, n_samp - 1 + group - 1)
    halo_send(pad, hs1, hr1)
    halo_zero(pad)
    halo_zero(dpad)
    for g in range(9):
        for c in range(3):
            block = w_ref[g * 3 + c]
            wt[g * cin:(g + 1) * cin, c * cout:(c + 1) * cout] = block
            wb[c * cin:(c + 1) * cin, g * cout:(g + 1) * cout] = block
    up_s[...] = up_ref[...].astype(F32)
    col[9 * cin:, :] = jnp.ones((16, cells * depth), BF16)
    bias = bias_ref[...]
    lane = lax.broadcasted_iota(jnp.int32, (cout, depth), 1)
    lane_i = lax.broadcasted_iota(jnp.int32, (cin, depth), 1)

    def ahead(v, lanes):
        return jnp.where(lanes < depth - 1, pltpu.roll(v, depth - 1, 1), 0.0)

    def behind(v, lanes):
        return jnp.where(lanes > 0, pltpu.roll(v, 1, 1), 0.0)

    halo_recv(pad, hs1, hr1)
    for x in range(rows):
        for y in range(cols):
            n = x * cols + y
            for a in range(3):
                for b in range(3):
                    g = a * 3 + b
                    col[g * cin:(g + 1) * cin, n * depth:(n + 1) * depth] = pad[x + a, y + b]

    step = 2 if cells % 2 == 0 else 1
    for m in range(0, cells, step):
        rhs = col[0:9 * cin, m * depth:(m + step) * depth]
        out = lax.dot_general(wt[...], rhs, (((0,), (0,)), ((), ())), preferred_element_type=F32)
        for n in range(m, m + step):
            k = (n - m) * depth
            y0, y1, y2 = (out[c * cout:(c + 1) * cout, k:k + depth] for c in range(3))
            pre = behind(y0, lane) + y1 + ahead(y2, lane) + bias
            t = jnp.exp(-jnp.abs(pre))
            soft = jnp.maximum(pre, 0.0) + jnp.log1p(t)
            sig = jnp.where(pre >= 0, 1.0, t) / (1.0 + t)
            act_s[pl.ds(n, cout, stride=cells), :] = 0.3 * pre + 0.7 * soft
            up = up_s[pl.ds(n, cout, stride=cells), :]
            d16 = (up * (0.3 + 0.7 * sig)).astype(BF16)
            dpad[1 + n // cols, 1 + n % cols] = d16
            d = d16.astype(F32)
            sd[0:cout, n * depth:(n + 1) * depth] = ahead(d, lane).astype(BF16)
            sd[cout:2 * cout, n * depth:(n + 1) * depth] = d16
            sd[2 * cout:, n * depth:(n + 1) * depth] = behind(d, lane).astype(BF16)
    halo_send(dpad, hs2, hr2)

    dw = lax.dot_general(col[...], sd[...], (((1,), (1,)), ((), ())), preferred_element_type=F32)
    k9, o2, half = 9 * cin, 2 * cout, 5 * cin
    stage[k9 + half - cin:, :] = jnp.zeros_like(stage[k9 + half - cin:, :])
    stage[0:k9, :] = dw[0:k9, 0:o2]
    stage[k9:k9 + half, 0:cout] = dw[0:half, o2:]
    stage[k9:k9 + k9 - half, cout:] = dw[half:k9, o2:]
    brow = k9 + k9 - half
    stage[brow:brow + 16, cout:] = dw[k9:, cout:o2]
    for q in range(owners):
        part[q] = stage[q * crows:(q + 1) * crows, :].astype(BF16)

    def when(cond, fn, always):
        if always:
            fn()
        else:
            pl.when(cond)(fn)

    every = owners == n_samp
    mine = me < owners

    def rs(src, dst, p):
        return pltpu.make_async_remote_copy(
            src_ref=part.at[src], dst_ref=r1.at[dst], send_sem=s1.at[src], recv_sem=v1.at[dst],
            device_id={"samp": p}, device_id_type=MESH,
        )

    def rs_start(k):
        p = lax.rem(me + k, n_samp)
        when(p < owners, lambda: rs(p, me, p).start(), every)

    def rs_sent(k):
        p = lax.rem(me + k, n_samp)
        when(p < owners, lambda: rs(p, me, p).wait_send(), every)

    each(n_samp, rs_start)
    act_ref[...] = act_s[...].astype(BF16)

    halo_recv(dpad, hs2, hr2)
    for x in range(rows):
        for y in range(cols):
            n = x * cols + y
            for a in range(3):
                for b in range(3):
                    g = a * 3 + b
                    dcol[g * cout:(g + 1) * cout, n * depth:(n + 1) * depth] = dpad[x + 2 - a, y + 2 - b]

    def backward(lo, hi):
        for m in range(lo, hi, step):
            out = jnp.dot(wb[...], dcol[:, m * depth:(m + step) * depth], preferred_element_type=F32)
            for n in range(m, m + step):
                k = (n - m) * depth
                u0, u1, u2 = (out[c * cin:(c + 1) * cin, k:k + depth] for c in range(3))
                ig_s[pl.ds(n, cin, stride=cells), :] = ahead(u0, lane_i) + u1 + behind(u2, lane_i)

    def gs(k):
        g, dev = group_id(k)
        return pltpu.make_async_remote_copy(
            src_ref=r2.at[gid], dst_ref=r2.at[gid], send_sem=s2.at[g], recv_sem=v2.at[gid],
            device_id=dev, device_id_type=MESH,
        )

    def gs_from(k):
        g, dev = group_id(k)
        return pltpu.make_async_remote_copy(
            src_ref=r2.at[g], dst_ref=r2.at[g], send_sem=s2.at[g], recv_sem=v2.at[g],
            device_id=dev, device_id_type=MESH,
        )

    def reduce_own():
        each(n_samp, lambda k: rs(0, lax.rem(me + k, n_samp), 0).wait_recv())
        r1[me] = part[me]
        total = lax.fori_loop(1, n_samp, lambda j, t: t + r1[j].astype(F32), r1[0].astype(F32))
        r2[gid] = total.astype(BF16)
        each(group, lambda k: gs(k).start())

    def ag(slot, p, sem):
        return pltpu.make_async_remote_copy(
            src_ref=gat.at[slot], dst_ref=gat.at[slot], send_sem=s3.at[sem], recv_sem=v3.at[slot],
            device_id={"samp": p}, device_id_type=MESH,
        )

    def ag_start(k):
        p = lax.rem(me + k, n_samp)
        ag(me, p, p).start()

    def gather_own():
        each(group, lambda k: gs_from(k).wait_recv())
        total = r2[0].astype(F32)
        for j in range(1, group):
            total = total + r2[j].astype(F32)
        gat[me] = total.astype(BF16)
        each(n_samp, ag_start)

    backward(0, cells)
    when(mine, reduce_own, every)
    ig_ref[...] = ig_s[...].astype(BF16)
    when(mine, gather_own, every)

    def ag_recv(k):
        p = lax.rem(me + k, n_samp)
        when(p < owners, lambda: ag(p, p, p).wait_recv(), every)

    each(n_samp, ag_recv)
    for q in range(owners):
        stage[q * crows:(q + 1) * crows, :] = gat[q].astype(F32) * norm
    for g in range(9):
        lo = g * cin
        wg_ref[g * 3] = stage[lo:lo + cin, 0:cout]
        wg_ref[g * 3 + 1] = stage[lo:lo + cin, cout:]
        if g < 5:
            wg_ref[g * 3 + 2] = stage[k9 + lo:k9 + lo + cin, 0:cout]
        else:
            wg_ref[g * 3 + 2] = stage[k9 + lo - half:k9 + lo - half + cin, cout:]
    bg_ref[...] = stage[brow:brow + 1, cout:]

    halo_sent(pad, hs1, hr1)
    halo_sent(dpad, hs2, hr2)
    each(n_samp, rs_sent)

    def own_sent():
        each(group, lambda k: gs(k).wait_send())
        each(n_samp, lambda k: ag(me, lax.rem(me + k, n_samp), lax.rem(me + k, n_samp)).wait_send())

    when(mine, own_sent, every)


def per_device(volume, kern, bias, upstream):
    samples, cin, rows, cols, depth = volume.shape
    cout = kern.shape[0]
    sizes = tuple(lax.axis_size(a) for a in ("samp", "sx", "sy"))
    cells = rows * cols
    packed = 14 * cin
    owners = min(sizes[0], 7)
    crows = -(-packed // (owners * 16)) * 16
    norm = 1.0 / math.sqrt(sizes[0] * samples * sizes[1] * sizes[2] * cells * depth)
    group = sizes[1] * sizes[2]
    dma = pltpu.SemaphoreType.DMA
    v = pltpu.VMEM
    whole = pl.BlockSpec(memory_space=pltpu.VMEM)
    w = kern.transpose(2, 3, 4, 1, 0).reshape(27, cin, cout)
    act, ig, wg, bg = pl.pallas_call(
        functools.partial(kernel, (rows, cols, cin, cout, depth), sizes, (owners, crows), norm),
        out_shape=(
            jax.ShapeDtypeStruct((cout * cells, depth), BF16),
            jax.ShapeDtypeStruct((cin * cells, depth), BF16),
            jax.ShapeDtypeStruct((27, cin, cout), F32),
            jax.ShapeDtypeStruct((1, cout), F32),
        ),
        in_specs=[whole] * 4,
        out_specs=[whole] * 4,
        scratch_shapes=[
            v((cin * cells, depth), F32), v((cout * cells, depth), F32),
            v((cout * cells, depth), F32), v((cin * cells, depth), F32),
            v((rows + 2, cols + 2, cin, depth), BF16), v((rows + 2, cols + 2, cout, depth), BF16),
            v((9 * cin + 16, cells * depth), BF16), v((9 * cout, cells * depth), BF16),
            v((3 * cout, cells * depth), BF16),
            v((9 * cin, 3 * cout), BF16), v((3 * cin, 9 * cout), BF16),
            v((owners * crows, 2 * cout), F32), v((owners, crows, 2 * cout), BF16),
            v((sizes[0], crows, 2 * cout), BF16), v((group, crows, 2 * cout), BF16),
            v((owners, crows, 2 * cout), BF16),
            dma((8,)), dma((8,)), dma((8,)), dma((8,)),
            dma((owners,)), dma((sizes[0],)), dma((group,)), dma((group,)),
            dma((sizes[0],)), dma((owners,)),
        ],
        compiler_params=pltpu.CompilerParams(
            collective_id=0, has_side_effects=True, vmem_limit_bytes=40 << 20
        ),
    )(
        volume.reshape(cin * cells, depth), w, bias.reshape(cout, 1), upstream.reshape(cout * cells, depth)
    )
    shape = (samples, -1, rows, cols, depth)
    filt = wg.reshape(3, 3, 3, cin, cout).transpose(4, 3, 0, 1, 2)
    return act.reshape(shape), ig.reshape(shape), filt, bg.reshape(cout)


def solution(mesh):
    block = P("samp", None, "sx", "sy", None)
    return jax.shard_map(
        per_device, mesh=mesh, in_specs=(block, P(), P(), block),
        out_specs=(block, block, P(), P()), check_vma=False,
    )
```

```python
import functools
import math

import jax
import jax.numpy as jnp
from jax import lax
from jax.experimental import pallas as pl
from jax.experimental.pallas import tpu as pltpu
from jax.sharding import PartitionSpec as P

MESH = pl.DeviceIdType.MESH
F32 = jnp.float32
BF16 = jnp.bfloat16
DIRS = tuple((dx, dy) for dx in (-1, 0, 1) for dy in (-1, 0, 1) if dx or dy)


def each(count, fn):
    if count <= 8:
        for k in range(1, count):
            fn(k)
    else:
        lax.fori_loop(1, count, lambda k, c: (fn(k), c)[1], 0)


def span(step, size):
    if step > 0:
        return pl.ds(size, 1), pl.ds(0, 1), pl.ds(size + 1, 1)
    if step < 0:
        return pl.ds(1, 1), pl.ds(size + 1, 1), pl.ds(0, 1)
    return pl.ds(1, size), pl.ds(1, size), pl.ds(1, size)


def taps(step):
    return {1: (2,), -1: (0,), 0: (0, 1, 2)}[step]


def places(step, size):
    return {1: (size + 1,), -1: (0,), 0: tuple(range(1, size + 1))}[step]


def kernel(
    dims, sizes, chunk, norm,
    vol_hbm, w_hbm, bias_hbm, up_hbm,
    act_ref, ig_ref, gat,
    vol_ref, w_ref, bias_ref, up_ref,
    vol_s, up_s, act_s, ig_s, pad, dpad, hout, hin, col, dcol, sd, wt, wtt, wb, wbs, stage, part, r1, r2,
    ls, hs1, hr1, hs2, hr2, s1, v1, s2, v2, s3, v3,
):
    rows, cols, cin, cout, depth = dims
    n_samp, n_sx, n_sy = sizes
    owners, crows = chunk
    cells = rows * cols
    group = n_sx * n_sy
    me = lax.axis_index("samp")
    ix, iy = lax.axis_index("sx"), lax.axis_index("sy")
    gid = ix * n_sy + iy

    loads = [
        pltpu.make_async_copy(src, dst, ls.at[i])
        for i, (src, dst) in enumerate(
            ((vol_hbm, vol_ref), (w_hbm, w_ref), (bias_hbm, bias_ref), (up_hbm, up_ref))
        )
    ]
    for load in loads:
        load.start()
    barrier = pltpu.get_barrier_semaphore()

    def greet_samp(k):
        pl.semaphore_signal(barrier, inc=1, device_id={"samp": lax.rem(me + k, n_samp)}, device_id_type=MESH)

    def group_id(k):
        g = lax.rem(gid + k, group)
        return g, {"sx": lax.div(g, n_sy), "sy": lax.rem(g, n_sy)}

    def greet_group(k):
        pl.semaphore_signal(barrier, inc=1, device_id=group_id(k)[1], device_id_type=MESH)

    each(n_samp, greet_samp)
    each(group, greet_group)

    def has(dx, dy):
        ok = None
        for i, step, size in ((ix, dx, n_sx), (iy, dy, n_sy)):
            if step:
                one = (i + 1 < size) if step > 0 else (i > 0)
                ok = one if ok is None else jnp.logical_and(ok, one)
        return ok

    def halo(buf, ss, rs, d):
        dx, dy = DIRS[d]
        sx, tx, ox = span(dx, rows)
        sy, ty, oy = span(dy, cols)
        src = buf.at[sx, sy] if buf is pad else hout.at[ox, oy]
        return pltpu.make_async_remote_copy(
            src_ref=src, dst_ref=buf.at[tx, ty],
            send_sem=ss.at[d], recv_sem=rs.at[d],
            device_id={"sx": ix + dx, "sy": iy + dy}, device_id_type=MESH,
        )

    live = [d for d, (dx, dy) in enumerate(DIRS) if not ((dx and n_sx == 1) or (dy and n_sy == 1))]

    def halo_zero(buf):
        for d, (dx, dy) in enumerate(DIRS):
            _, tx, _ = span(dx, rows)
            _, ty, _ = span(dy, cols)

            def clear():
                v = buf[tx, ty]
                buf[tx, ty] = jnp.zeros_like(v)

            if d in live:
                pl.when(jnp.logical_not(has(-dx, -dy)))(clear)
            else:
                clear()

    def halo_send(buf, ss, rs):
        for d in live:
            pl.when(has(*DIRS[d]))(lambda: halo(buf, ss, rs, d).start())

    def halo_recv(buf, ss, rs):
        for d in live:
            dx, dy = DIRS[d]
            pl.when(has(-dx, -dy))(lambda: halo(buf, ss, rs, d).wait_recv())

    def halo_sent(buf, ss, rs):
        for d in live:
            pl.when(has(*DIRS[d]))(lambda: halo(buf, ss, rs, d).wait_send())

    loads[0].wait()
    vol_s[...] = vol_ref[...].astype(F32)
    for x in range(rows):
        for y in range(cols):
            pad[1 + x, 1 + y] = vol_s[pl.ds(x * cols + y, cin, stride=cells), :].astype(BF16)
    pl.semaphore_wait(barrier, n_samp - 1 + group - 1)
    halo_send(pad, hs1, hr1)
    halo_zero(pad)
    halo_zero(hin)
    for x in (0, rows + 1):
        dpad[x] = jnp.zeros((cols + 2, cout, depth), BF16)
    for x in range(1, rows + 1):
        for y in (0, cols + 1):
            dpad[x, y] = jnp.zeros((cout, depth), BF16)
    for load in loads[1:]:
        load.wait()
    for g in range(9):
        for c in range(3):
            block = w_ref[g * 3 + c]
            wt[g * cin:(g + 1) * cin, c * cout:(c + 1) * cout] = block
            wb[c * cin:(c + 1) * cin, g * cout:(g + 1) * cout] = block
            wbs[g, c * cin:(c + 1) * cin, :] = block
    wtt[...] = wt[...].T
    up_s[...] = up_ref[...].astype(F32)
    col[9 * cin:, :] = jnp.ones((16, cells * depth), BF16)
    eye = lax.broadcasted_iota(jnp.int32, (cout, cout), 0) == lax.broadcasted_iota(jnp.int32, (cout, cout), 1)
    bias = jnp.sum(jnp.where(eye, bias_ref[...], 0.0), axis=1, keepdims=True)
    lane = lax.broadcasted_iota(jnp.int32, (cout, depth), 1)
    lane_i = lax.broadcasted_iota(jnp.int32, (cin, depth), 1)

    def ahead(v, lanes):
        return jnp.where(lanes < depth - 1, pltpu.roll(v, depth - 1, 1), 0.0)

    def behind(v, lanes):
        return jnp.where(lanes > 0, pltpu.roll(v, 1, 1), 0.0)

    halo_recv(pad, hs1, hr1)
    for x in range(rows):
        for y in range(cols):
            n = x * cols + y
            for a in range(3):
                for b in range(3):
                    g = a * 3 + b
                    col[g * cin:(g + 1) * cin, n * depth:(n + 1) * depth] = pad[x + a, y + b]

    step = 2 if cells % 2 == 0 else 1
    for m in range(0, cells, step):
        rhs = col[0:9 * cin, m * depth:(m + step) * depth]
        out = jnp.dot(wtt[...], rhs, preferred_element_type=F32)
        for n in range(m, m + step):
            k = (n - m) * depth
            y0, y1, y2 = (out[c * cout:(c + 1) * cout, k:k + depth] for c in range(3))
            pre = behind(y0, lane) + y1 + ahead(y2, lane) + bias
            t = jnp.exp(-jnp.abs(pre))
            one = 1.0 + t
            soft = jnp.maximum(pre, 0.0) + jnp.log(one)
            sig = jnp.where(pre >= 0, 1.0, t) / one
            act_s[pl.ds(n, cout, stride=cells), :] = 0.3 * pre + 0.7 * soft
            up = up_s[pl.ds(n, cout, stride=cells), :]
            d16 = (up * (0.3 + 0.7 * sig)).astype(BF16)
            dpad[1 + n // cols, 1 + n % cols] = d16
            d = d16.astype(F32)
            sd[0:cout, n * depth:(n + 1) * depth] = ahead(d, lane).astype(BF16)
            sd[cout:2 * cout, n * depth:(n + 1) * depth] = d16
            sd[2 * cout:, n * depth:(n + 1) * depth] = behind(d, lane).astype(BF16)

    dw = lax.dot_general(col[...], sd[...], (((1,), (1,)), ((), ())), preferred_element_type=F32)
    k9, o2, half = 9 * cin, 2 * cout, 5 * cin
    stage[k9 + half - cin:, :] = jnp.zeros_like(stage[k9 + half - cin:, :])
    stage[0:k9, :] = dw[0:k9, 0:o2]
    stage[k9:k9 + half, 0:cout] = dw[0:half, o2:]
    stage[k9:k9 + k9 - half, cout:] = dw[half:k9, o2:]
    brow = k9 + k9 - half
    stage[brow:brow + 16, cout:] = dw[k9:, cout:o2]
    for q in range(owners):
        part[q] = stage[q * crows:(q + 1) * crows, :].astype(BF16)

    def when(cond, fn, always):
        if always:
            fn()
        else:
            pl.when(cond)(fn)

    every = owners == n_samp
    mine = me < owners

    def rs(src, dst, p):
        return pltpu.make_async_remote_copy(
            src_ref=part.at[src], dst_ref=r1.at[dst], send_sem=s1.at[src], recv_sem=v1.at[dst],
            device_id={"samp": p}, device_id_type=MESH,
        )

    def rs_start(k):
        p = lax.rem(me + k, n_samp)
        when(p < owners, lambda: rs(p, me, p).start(), every)

    def rs_sent(k):
        p = lax.rem(me + k, n_samp)
        when(p < owners, lambda: rs(p, me, p).wait_send(), every)

    each(n_samp, rs_start)

    def outside(d):
        dx, dy = DIRS[d]
        spots = [(x, y) for x in places(dx, rows) for y in places(dy, cols)]
        for m in range(0, len(spots), 2):
            pair = spots[m:m + 2]
            out = None
            for a in taps(dx):
                for b in taps(dy):
                    rhs = jnp.concatenate([dpad[x + 1 - a, y + 1 - b] for x, y in pair], axis=1)
                    term = jnp.dot(wbs[a * 3 + b], rhs, preferred_element_type=F32)
                    out = term if out is None else out + term
            for n, (x, y) in enumerate(pair):
                u0, u1, u2 = (out[c * cin:(c + 1) * cin, n * depth:(n + 1) * depth] for c in range(3))
                hout[x, y] = (ahead(u0, lane_i) + u1 + behind(u2, lane_i)).astype(BF16)
        halo(hin, hs2, hr2, d).start()

    for d in live:
        pl.when(has(*DIRS[d]))(lambda: outside(d))
    act_ref[...] = act_s[...].astype(BF16)
    for x in range(rows):
        for y in range(cols):
            n = x * cols + y
            for a in range(3):
                for b in range(3):
                    g = a * 3 + b
                    dcol[g * cout:(g + 1) * cout, n * depth:(n + 1) * depth] = dpad[x + 2 - a, y + 2 - b]

    def backward(lo, hi):
        for m in range(lo, hi, step):
            out = jnp.dot(wb[...], dcol[:, m * depth:(m + step) * depth], preferred_element_type=F32)
            for n in range(m, m + step):
                k = (n - m) * depth
                u0, u1, u2 = (out[c * cin:(c + 1) * cin, k:k + depth] for c in range(3))
                ig_s[pl.ds(n, cin, stride=cells), :] = ahead(u0, lane_i) + u1 + behind(u2, lane_i)

    def gs(k):
        g, dev = group_id(k)
        return pltpu.make_async_remote_copy(
            src_ref=r2.at[gid], dst_ref=r2.at[gid], send_sem=s2.at[g], recv_sem=v2.at[gid],
            device_id=dev, device_id_type=MESH,
        )

    def gs_from(k):
        g, dev = group_id(k)
        return pltpu.make_async_remote_copy(
            src_ref=r2.at[g], dst_ref=r2.at[g], send_sem=s2.at[g], recv_sem=v2.at[g],
            device_id=dev, device_id_type=MESH,
        )

    def reduce_own():
        each(n_samp, lambda k: rs(0, lax.rem(me + k, n_samp), 0).wait_recv())
        r1[me] = part[me]
        total = lax.fori_loop(1, n_samp, lambda j, t: t + r1[j].astype(F32), r1[0].astype(F32))
        r2[gid] = total.astype(BF16)
        each(group, lambda k: gs(k).start())

    def ag(slot, p, sem):
        return pltpu.make_async_remote_copy(
            src_ref=gat.at[slot], dst_ref=gat.at[slot], send_sem=s3.at[sem], recv_sem=v3.at[slot],
            device_id={"samp": p}, device_id_type=MESH,
        )

    def ag_start(k):
        p = lax.rem(me + k, n_samp)
        ag(me, p, p).start()

    def gather_own():
        each(group, lambda k: gs_from(k).wait_recv())
        total = r2[0].astype(F32)
        for j in range(1, group):
            total = total + r2[j].astype(F32)
        gat[me] = total.astype(BF16)
        each(n_samp, ag_start)

    backward(0, cells)
    when(mine, reduce_own, every)
    halo_recv(hin, hs2, hr2)
    for x in range(1, rows + 1):
        for y in range(1, cols + 1):
            spots = []
            for dx in (-1, 0, 1):
                for dy in (-1, 0, 1):
                    if (dx or dy) and (not dx or x == (1 if dx < 0 else rows)) and (not dy or y == (1 if dy < 0 else cols)):
                        spots.append((x + dx, y + dy))
            if spots:
                at = pl.ds((x - 1) * cols + y - 1, cin, stride=cells)
                total = ig_s[at, :]
                for spot in spots:
                    total = total + hin[spot].astype(F32)
                ig_s[at, :] = total
    ig_ref[...] = ig_s[...].astype(BF16)
    when(mine, gather_own, every)

    def ag_recv(k):
        p = lax.rem(me + k, n_samp)
        when(p < owners, lambda: ag(p, p, p).wait_recv(), every)

    each(n_samp, ag_recv)
    halo_sent(pad, hs1, hr1)
    halo_sent(hin, hs2, hr2)
    each(n_samp, rs_sent)

    def own_sent():
        each(group, lambda k: gs(k).wait_send())
        each(n_samp, lambda k: ag(me, lax.rem(me + k, n_samp), lax.rem(me + k, n_samp)).wait_send())

    when(mine, own_sent, every)


def finish(norm, cin, cout, act_ref, ig_ref, gat, act_hbm, ig_hbm, wg_hbm, bg_hbm, stage, wg_ref, bg_ref, sem):
    copies = [
        pltpu.make_async_copy(src, dst, sem.at[i])
        for i, (src, dst) in enumerate(
            ((act_ref, act_hbm), (ig_ref, ig_hbm), (wg_ref, wg_hbm), (bg_ref, bg_hbm))
        )
    ]
    copies[0].start()
    copies[1].start()
    owners, crows, _ = gat.shape
    k9, half = 9 * cin, 5 * cin
    for q in range(owners):
        stage[q * crows:(q + 1) * crows, :] = gat[q].astype(F32) * norm
    for g in range(9):
        lo = g * cin
        wg_ref[g * 3] = stage[lo:lo + cin, 0:cout]
        wg_ref[g * 3 + 1] = stage[lo:lo + cin, cout:]
        if g < 5:
            wg_ref[g * 3 + 2] = stage[k9 + lo:k9 + lo + cin, 0:cout]
        else:
            wg_ref[g * 3 + 2] = stage[k9 + lo - half:k9 + lo - half + cin, cout:]
    brow = k9 + k9 - half
    bg_ref[...] = stage[brow:brow + 1, cout:]
    copies[2].start()
    copies[3].start()
    for copy in copies:
        copy.wait()


def per_device(volume, kern, bias, upstream):
    samples, cin, rows, cols, depth = volume.shape
    cout = kern.shape[0]
    sizes = tuple(lax.axis_size(a) for a in ("samp", "sx", "sy"))
    cells = rows * cols
    packed = 14 * cin
    owners = min(sizes[0], 7)
    crows = -(-packed // (owners * 16)) * 16
    norm = 1.0 / math.sqrt(sizes[0] * samples * sizes[1] * sizes[2] * cells * depth)
    group = sizes[1] * sizes[2]
    dma = pltpu.SemaphoreType.DMA
    v = pltpu.VMEM
    whole = pl.BlockSpec(memory_space=pltpu.VMEM)
    w = kern.transpose(2, 3, 4, 1, 0).reshape(27, cin, cout)
    hbm = pl.BlockSpec(memory_space=pltpu.HBM)
    act_out = jax.ShapeDtypeStruct((cout * cells, depth), BF16)
    ig_out = jax.ShapeDtypeStruct((cin * cells, depth), BF16)
    wg_out = jax.ShapeDtypeStruct((27, cin, cout), F32)
    bg_out = jax.ShapeDtypeStruct((1, cout), F32)
    act, ig, gat = pl.pallas_call(
        functools.partial(kernel, (rows, cols, cin, cout, depth), sizes, (owners, crows), norm),
        out_shape=(act_out, ig_out, jax.ShapeDtypeStruct((owners, crows, 2 * cout), BF16)),
        in_specs=[hbm] * 4,
        out_specs=[whole] * 3,
        scratch_shapes=[
            v((cin * cells, depth), BF16), v((27, cin, cout), BF16), v((1, cout), F32), v((cout * cells, depth), BF16),
            v((cin * cells, depth), F32), v((cout * cells, depth), F32),
            v((cout * cells, depth), F32), v((cin * cells, depth), F32),
            v((rows + 2, cols + 2, cin, depth), BF16), v((rows + 2, cols + 2, cout, depth), BF16),
            v((rows + 2, cols + 2, cin, depth), BF16), v((rows + 2, cols + 2, cin, depth), BF16),
            v((9 * cin + 16, cells * depth), BF16), v((9 * cout, cells * depth), BF16),
            v((3 * cout, cells * depth), BF16),
            v((9 * cin, 3 * cout), BF16), v((3 * cout, 9 * cin), BF16), v((3 * cin, 9 * cout), BF16),
            v((9, 3 * cin, cout), BF16),
            v((owners * crows, 2 * cout), F32), v((owners, crows, 2 * cout), BF16),
            v((sizes[0], crows, 2 * cout), BF16), v((group, crows, 2 * cout), BF16),
            dma((4,)), dma((8,)), dma((8,)), dma((8,)), dma((8,)),
            dma((owners,)), dma((sizes[0],)), dma((group,)), dma((group,)),
            dma((sizes[0],)), dma((owners,)),
        ],
        compiler_params=pltpu.CompilerParams(
            collective_id=0, has_side_effects=True, vmem_limit_bytes=40 << 20
        ),
    )(
        *(
            pltpu.with_memory_space_constraint(x, pltpu.HBM)
            for x in (
                volume.reshape(cin * cells, depth), w, bias.reshape(1, cout), upstream.reshape(cout * cells, depth)
            )
        )
    )
    act, ig, wg, bg = pl.pallas_call(
        functools.partial(finish, norm, cin, cout),
        out_shape=(act_out, ig_out, wg_out, bg_out),
        in_specs=[whole] * 3,
        out_specs=[hbm] * 4,
        scratch_shapes=[v((owners * crows, 2 * cout), F32), v((27, cin, cout), F32), v((1, cout), F32), dma((4,))],
        compiler_params=pltpu.CompilerParams(vmem_limit_bytes=16 << 20),
    )(act, ig, gat)
    shape = (samples, -1, rows, cols, depth)
    filt = wg.reshape(3, 3, 3, cin, cout).transpose(4, 3, 0, 1, 2)
    return act.reshape(shape), ig.reshape(shape), filt, bg.reshape(cout)


def solution(mesh):
    block = P("samp", None, "sx", "sy", None)
    return jax.shard_map(
        per_device, mesh=mesh, in_specs=(block, P(), P(), block),
        out_specs=(block, block, P(), P()), check_vma=False,
    )
```

```python
import functools
import math

import jax
import jax.numpy as jnp
from jax import lax
from jax.experimental import pallas as pl
from jax.experimental.pallas import tpu as pltpu
from jax.sharding import PartitionSpec as P

MESH = pl.DeviceIdType.MESH
F32 = jnp.float32
BF16 = jnp.bfloat16
DIRS = tuple((dx, dy) for dx in (-1, 0, 1) for dy in (-1, 0, 1) if dx or dy)


def each(count, fn):
    if count <= 8:
        for k in range(1, count):
            fn(k)
    else:
        lax.fori_loop(1, count, lambda k, c: (fn(k), c)[1], 0)


def span(step, size):
    if step > 0:
        return pl.ds(size, 1), pl.ds(0, 1), pl.ds(size + 1, 1)
    if step < 0:
        return pl.ds(1, 1), pl.ds(size + 1, 1), pl.ds(0, 1)
    return pl.ds(1, size), pl.ds(1, size), pl.ds(1, size)


def taps(step):
    return {1: (2,), -1: (0,), 0: (0, 1, 2)}[step]


def places(step, size):
    return {1: (size + 1,), -1: (0,), 0: tuple(range(1, size + 1))}[step]


def kernel(
    dims, sizes, chunk, norm,
    vol_hbm, w_hbm, bias_hbm, up_hbm,
    act_ref, ig_ref, gat,
    vol_ref, w_ref, bias_ref, up_ref,
    vol_s, up_s, act_s, ig_s, pad, dpad, hout, hin, col, ys, dcol, sd, wt, wtt, wb, wbs, stage, part, r1, r2,
    ls, hs1, hr1, hs2, hr2, s1, v1, s2, v2, s3, v3,
):
    rows, cols, cin, cout, depth = dims
    n_samp, n_sx, n_sy = sizes
    owners, crows = chunk
    cells = rows * cols
    group = n_sx * n_sy
    me = lax.axis_index("samp")
    ix, iy = lax.axis_index("sx"), lax.axis_index("sy")
    gid = ix * n_sy + iy

    loads = [
        pltpu.make_async_copy(src, dst, ls.at[i])
        for i, (src, dst) in enumerate(
            ((vol_hbm, vol_ref), (w_hbm, w_ref), (bias_hbm, bias_ref), (up_hbm, up_ref))
        )
    ]
    for load in loads:
        load.start()
    barrier = pltpu.get_barrier_semaphore()

    def greet_samp(k):
        pl.semaphore_signal(barrier, inc=1, device_id={"samp": lax.rem(me + k, n_samp)}, device_id_type=MESH)

    def group_id(k):
        g = lax.rem(gid + k, group)
        return g, {"sx": lax.div(g, n_sy), "sy": lax.rem(g, n_sy)}

    def greet_group(k):
        pl.semaphore_signal(barrier, inc=1, device_id=group_id(k)[1], device_id_type=MESH)

    each(n_samp, greet_samp)
    each(group, greet_group)

    def has(dx, dy):
        ok = None
        for i, step, size in ((ix, dx, n_sx), (iy, dy, n_sy)):
            if step:
                one = (i + 1 < size) if step > 0 else (i > 0)
                ok = one if ok is None else jnp.logical_and(ok, one)
        return ok

    half = cols // 2 if cols % 4 == 0 else cols

    def halo(buf, ss, rs, d, piece=0):
        dx, dy = DIRS[d]
        sx, tx, ox = span(dx, rows)
        sy, ty, oy = span(dy, cols)
        if buf is pad and not dy and half < cols:
            sy = ty = pl.ds(half + 2, cols - half - 1) if piece else pl.ds(1, half + 1)
        sem = d + 8 * piece
        src = buf.at[sx, sy] if buf is pad else hout.at[ox, oy]
        return pltpu.make_async_remote_copy(
            src_ref=src, dst_ref=buf.at[tx, ty],
            send_sem=ss.at[sem], recv_sem=rs.at[sem],
            device_id={"sx": ix + dx, "sy": iy + dy}, device_id_type=MESH,
        )

    live = [d for d, (dx, dy) in enumerate(DIRS) if not ((dx and n_sx == 1) or (dy and n_sy == 1))]

    def halo_zero(buf):
        for d, (dx, dy) in enumerate(DIRS):
            _, tx, _ = span(dx, rows)
            _, ty, _ = span(dy, cols)

            def clear():
                v = buf[tx, ty]
                buf[tx, ty] = jnp.zeros_like(v)

            if d in live:
                pl.when(jnp.logical_not(has(-dx, -dy)))(clear)
            else:
                clear()

    late = [d for d in live if not DIRS[d][1]] if half < cols else []
    near = sorted(live, key=lambda d: (d in late, DIRS[d][1] == 0))

    def halo_send(buf, ss, rs):
        for d in near:
            pl.when(has(*DIRS[d]))(lambda: halo(buf, ss, rs, d).start())
        for d in late:
            pl.when(has(*DIRS[d]))(lambda: halo(buf, ss, rs, d, 1).start())

    def halo_recv(buf, ss, rs, which, piece=0):
        for d in which:
            dx, dy = DIRS[d]
            pl.when(has(-dx, -dy))(lambda: halo(buf, ss, rs, d, piece).wait_recv())

    def halo_sent(buf, ss, rs, which, piece=0):
        for d in which:
            pl.when(has(*DIRS[d]))(lambda: halo(buf, ss, rs, d, piece).wait_send())

    loads[0].wait()
    vol_s[...] = vol_ref[...].astype(F32)
    for x in range(rows):
        for y in range(cols):
            pad[1 + x, 1 + y] = vol_s[pl.ds(x * cols + y, cin, stride=cells), :].astype(BF16)
    pl.semaphore_wait(barrier, n_samp - 1 + group - 1)
    halo_send(pad, hs1, hr1)
    halo_zero(pad)
    halo_zero(hin)
    for x in (0, rows + 1):
        dpad[x] = jnp.zeros((cols + 2, cout, depth), BF16)
    for x in range(1, rows + 1):
        for y in (0, cols + 1):
            dpad[x, y] = jnp.zeros((cout, depth), BF16)
    for load in loads[1:]:
        load.wait()
    for g in range(9):
        for c in range(3):
            block = w_ref[g * 3 + c]
            wt[g * cin:(g + 1) * cin, c * cout:(c + 1) * cout] = block
            wb[c * cin:(c + 1) * cin, g * cout:(g + 1) * cout] = block
            wbs[g, c * cin:(c + 1) * cin, :] = block
    wtt[...] = wt[...].T
    up_s[...] = up_ref[...].astype(F32)
    col[9 * cin:, :] = jnp.ones((16, cells * depth), BF16)
    eye = lax.broadcasted_iota(jnp.int32, (cout, cout), 0) == lax.broadcasted_iota(jnp.int32, (cout, cout), 1)
    bias = jnp.sum(jnp.where(eye, bias_ref[...], 0.0), axis=1, keepdims=True)
    lane_i = lax.broadcasted_iota(jnp.int32, (cin, depth), 1)

    def ahead(v, lanes):
        return jnp.where(lanes < depth - 1, pltpu.roll(v, depth - 1, 1), 0.0)

    def behind(v, lanes):
        return jnp.where(lanes > 0, pltpu.roll(v, 1, 1), 0.0)

    step = 2 if cols % 2 == 0 else 1
    sub = cout // 2 if cout % 32 == 0 else cout

    def columns(lo, hi):
        for x in range(rows):
            for y in range(lo, hi):
                n = x * cols + y
                for a in range(3):
                    for b in range(3):
                        g = a * 3 + b
                        col[g * cin:(g + 1) * cin, n * depth:(n + 1) * depth] = pad[x + a, y + b]

    def product(m):
        at = slice(m * depth, (m + step) * depth)
        ys[:, at] = jnp.dot(wtt[...], col[0:9 * cin, at], preferred_element_type=F32)

    def pointwise(n, h):
        at = slice(n * depth, (n + 1) * depth)
        lane = lax.broadcasted_iota(jnp.int32, (sub, depth), 1)
        y0, y1, y2 = (ys[c * cout + h:c * cout + h + sub, at] for c in range(3))
        pre = behind(y0, lane) + y1 + ahead(y2, lane) + bias[h:h + sub]
        t = jnp.exp(-jnp.abs(pre))
        one = 1.0 + t
        soft = jnp.maximum(pre, 0.0) + jnp.log(one)
        sig = jnp.where(pre >= 0, 1.0, t) / one
        spot = pl.ds(h * cells + n, sub, stride=cells)
        act_s[spot, :] = 0.3 * pre + 0.7 * soft
        d16 = (up_s[spot, :] * (0.3 + 0.7 * sig)).astype(BF16)
        dpad[1 + n // cols, 1 + n % cols, h:h + sub, :] = d16
        d = d16.astype(F32)
        sd[h:h + sub, at] = ahead(d, lane).astype(BF16)
        sd[cout + h:cout + h + sub, at] = d16
        sd[2 * cout + h:2 * cout + h + sub, at] = behind(d, lane).astype(BF16)

    def forward(lo, hi):
        columns(lo, hi)
        ms = [x * cols + y for x in range(rows) for y in range(lo, hi, step)]
        product(ms[0])
        for i, m in enumerate(ms):
            if i + 1 < len(ms):
                product(ms[i + 1])
            for n in range(m, m + step):
                for h in range(0, cout, sub):
                    pointwise(n, h)

    halo_recv(pad, hs1, hr1, live)
    forward(0, half)
    if half < cols:
        halo_recv(pad, hs1, hr1, late, 1)
        forward(half, cols)

    dw = lax.dot_general(col[...], sd[...], (((1,), (1,)), ((), ())), preferred_element_type=F32)
    k9, o2, five = 9 * cin, 2 * cout, 5 * cin
    stage[k9 + five - cin:, :] = jnp.zeros_like(stage[k9 + five - cin:, :])
    stage[0:k9, :] = dw[0:k9, 0:o2]
    stage[k9:k9 + five, 0:cout] = dw[0:five, o2:]
    stage[k9:k9 + k9 - five, cout:] = dw[five:k9, o2:]
    brow = k9 + k9 - five
    stage[brow:brow + 16, cout:] = dw[k9:, cout:o2]
    for q in range(owners):
        part[q] = stage[q * crows:(q + 1) * crows, :].astype(BF16)

    def when(cond, fn, always):
        if always:
            fn()
        else:
            pl.when(cond)(fn)

    every = owners == n_samp
    mine = me < owners

    def rs(src, dst, p):
        return pltpu.make_async_remote_copy(
            src_ref=part.at[src], dst_ref=r1.at[dst], send_sem=s1.at[src], recv_sem=v1.at[dst],
            device_id={"samp": p}, device_id_type=MESH,
        )

    def rs_start(k):
        p = lax.rem(me + k, n_samp)
        when(p < owners, lambda: rs(p, me, p).start(), every)

    def rs_sent(k):
        p = lax.rem(me + k, n_samp)
        when(p < owners, lambda: rs(p, me, p).wait_send(), every)

    each(n_samp, rs_start)

    def outside(d):
        dx, dy = DIRS[d]
        spots = [(x, y) for x in places(dx, rows) for y in places(dy, cols)]
        for m in range(0, len(spots), 2):
            pair = spots[m:m + 2]
            out = None
            for a in taps(dx):
                for b in taps(dy):
                    rhs = jnp.concatenate([dpad[x + 1 - a, y + 1 - b] for x, y in pair], axis=1)
                    term = jnp.dot(wbs[a * 3 + b], rhs, preferred_element_type=F32)
                    out = term if out is None else out + term
            for n, (x, y) in enumerate(pair):
                u0, u1, u2 = (out[c * cin:(c + 1) * cin, n * depth:(n + 1) * depth] for c in range(3))
                hout[x, y] = (ahead(u0, lane_i) + u1 + behind(u2, lane_i)).astype(BF16)
        halo(hin, hs2, hr2, d).start()

    for d in live:
        pl.when(has(*DIRS[d]))(lambda: outside(d))
    act_ref[...] = act_s[...].astype(BF16)
    for x in range(rows):
        for y in range(cols):
            n = x * cols + y
            for a in range(3):
                for b in range(3):
                    g = a * 3 + b
                    dcol[g * cout:(g + 1) * cout, n * depth:(n + 1) * depth] = dpad[x + 2 - a, y + 2 - b]

    def backward(lo, hi):
        for m in range(lo, hi, step):
            out = jnp.dot(wb[...], dcol[:, m * depth:(m + step) * depth], preferred_element_type=F32)
            for n in range(m, m + step):
                k = (n - m) * depth
                u0, u1, u2 = (out[c * cin:(c + 1) * cin, k:k + depth] for c in range(3))
                ig_s[pl.ds(n, cin, stride=cells), :] = ahead(u0, lane_i) + u1 + behind(u2, lane_i)

    def gs(k):
        g, dev = group_id(k)
        return pltpu.make_async_remote_copy(
            src_ref=r2.at[gid], dst_ref=r2.at[gid], send_sem=s2.at[g], recv_sem=v2.at[gid],
            device_id=dev, device_id_type=MESH,
        )

    def gs_from(k):
        g, dev = group_id(k)
        return pltpu.make_async_remote_copy(
            src_ref=r2.at[g], dst_ref=r2.at[g], send_sem=s2.at[g], recv_sem=v2.at[g],
            device_id=dev, device_id_type=MESH,
        )

    def reduce_own():
        each(n_samp, lambda k: rs(0, lax.rem(me + k, n_samp), 0).wait_recv())
        r1[me] = part[me]
        total = lax.fori_loop(1, n_samp, lambda j, t: t + r1[j].astype(F32), r1[0].astype(F32))
        r2[gid] = total.astype(BF16)
        each(group, lambda k: gs(k).start())

    def ag(slot, p, sem):
        return pltpu.make_async_remote_copy(
            src_ref=gat.at[slot], dst_ref=gat.at[slot], send_sem=s3.at[sem], recv_sem=v3.at[slot],
            device_id={"samp": p}, device_id_type=MESH,
        )

    def ag_start(k):
        p = lax.rem(me + k, n_samp)
        ag(me, p, p).start()

    def gather_own():
        each(group, lambda k: gs_from(k).wait_recv())
        total = r2[0].astype(F32)
        for j in range(1, group):
            total = total + r2[j].astype(F32)
        gat[me] = total.astype(BF16)
        each(n_samp, ag_start)

    backward(0, cells)
    when(mine, reduce_own, every)
    halo_recv(hin, hs2, hr2, live)
    for x in range(1, rows + 1):
        for y in range(1, cols + 1):
            spots = []
            for dx in (-1, 0, 1):
                for dy in (-1, 0, 1):
                    if (dx or dy) and (not dx or x == (1 if dx < 0 else rows)) and (not dy or y == (1 if dy < 0 else cols)):
                        spots.append((x + dx, y + dy))
            if spots:
                at = pl.ds((x - 1) * cols + y - 1, cin, stride=cells)
                total = ig_s[at, :]
                for spot in spots:
                    total = total + hin[spot].astype(F32)
                ig_s[at, :] = total
    ig_ref[...] = ig_s[...].astype(BF16)
    when(mine, gather_own, every)

    def ag_recv(k):
        p = lax.rem(me + k, n_samp)
        when(p < owners, lambda: ag(p, p, p).wait_recv(), every)

    each(n_samp, ag_recv)
    halo_sent(pad, hs1, hr1, live)
    halo_sent(pad, hs1, hr1, late, 1)
    halo_sent(hin, hs2, hr2, live)
    each(n_samp, rs_sent)

    def own_sent():
        each(group, lambda k: gs(k).wait_send())
        each(n_samp, lambda k: ag(me, lax.rem(me + k, n_samp), lax.rem(me + k, n_samp)).wait_send())

    when(mine, own_sent, every)


def finish(norm, cin, cout, act_ref, ig_ref, gat, act_hbm, ig_hbm, wg_hbm, bg_hbm, stage, wg_ref, bg_ref, sem):
    copies = [
        pltpu.make_async_copy(src, dst, sem.at[i])
        for i, (src, dst) in enumerate(
            ((act_ref, act_hbm), (ig_ref, ig_hbm), (wg_ref, wg_hbm), (bg_ref, bg_hbm))
        )
    ]
    copies[0].start()
    copies[1].start()
    owners, crows, _ = gat.shape
    k9, half = 9 * cin, 5 * cin
    for q in range(owners):
        stage[q * crows:(q + 1) * crows, :] = gat[q].astype(F32) * norm
    for g in range(9):
        lo = g * cin
        wg_ref[g * 3] = stage[lo:lo + cin, 0:cout]
        wg_ref[g * 3 + 1] = stage[lo:lo + cin, cout:]
        if g < 5:
            wg_ref[g * 3 + 2] = stage[k9 + lo:k9 + lo + cin, 0:cout]
        else:
            wg_ref[g * 3 + 2] = stage[k9 + lo - half:k9 + lo - half + cin, cout:]
    brow = k9 + k9 - half
    bg_ref[...] = stage[brow:brow + 1, cout:]
    copies[2].start()
    copies[3].start()
    for copy in copies:
        copy.wait()


def per_device(volume, kern, bias, upstream):
    samples, cin, rows, cols, depth = volume.shape
    cout = kern.shape[0]
    sizes = tuple(lax.axis_size(a) for a in ("samp", "sx", "sy"))
    cells = rows * cols
    packed = 14 * cin
    owners = min(sizes[0], 7)
    crows = -(-packed // (owners * 16)) * 16
    norm = 1.0 / math.sqrt(sizes[0] * samples * sizes[1] * sizes[2] * cells * depth)
    group = sizes[1] * sizes[2]
    dma = pltpu.SemaphoreType.DMA
    v = pltpu.VMEM
    whole = pl.BlockSpec(memory_space=pltpu.VMEM)
    w = kern.transpose(2, 3, 4, 1, 0).reshape(27, cin, cout)
    hbm = pl.BlockSpec(memory_space=pltpu.HBM)
    act_out = jax.ShapeDtypeStruct((cout * cells, depth), BF16)
    ig_out = jax.ShapeDtypeStruct((cin * cells, depth), BF16)
    wg_out = jax.ShapeDtypeStruct((27, cin, cout), F32)
    bg_out = jax.ShapeDtypeStruct((1, cout), F32)
    act, ig, gat = pl.pallas_call(
        functools.partial(kernel, (rows, cols, cin, cout, depth), sizes, (owners, crows), norm),
        out_shape=(act_out, ig_out, jax.ShapeDtypeStruct((owners, crows, 2 * cout), BF16)),
        in_specs=[hbm] * 4,
        out_specs=[whole] * 3,
        scratch_shapes=[
            v((cin * cells, depth), BF16), v((27, cin, cout), BF16), v((1, cout), F32), v((cout * cells, depth), BF16),
            v((cin * cells, depth), F32), v((cout * cells, depth), F32),
            v((cout * cells, depth), F32), v((cin * cells, depth), F32),
            v((rows + 2, cols + 2, cin, depth), BF16), v((rows + 2, cols + 2, cout, depth), BF16),
            v((rows + 2, cols + 2, cin, depth), BF16), v((rows + 2, cols + 2, cin, depth), BF16),
            v((9 * cin + 16, cells * depth), BF16), v((3 * cout, cells * depth), F32), v((9 * cout, cells * depth), BF16),
            v((3 * cout, cells * depth), BF16),
            v((9 * cin, 3 * cout), BF16), v((3 * cout, 9 * cin), BF16), v((3 * cin, 9 * cout), BF16),
            v((9, 3 * cin, cout), BF16),
            v((owners * crows, 2 * cout), F32), v((owners, crows, 2 * cout), BF16),
            v((sizes[0], crows, 2 * cout), BF16), v((group, crows, 2 * cout), BF16),
            dma((4,)), dma((16,)), dma((16,)), dma((8,)), dma((8,)),
            dma((owners,)), dma((sizes[0],)), dma((group,)), dma((group,)),
            dma((sizes[0],)), dma((owners,)),
        ],
        compiler_params=pltpu.CompilerParams(
            collective_id=0, has_side_effects=True, vmem_limit_bytes=40 << 20
        ),
    )(
        *(
            pltpu.with_memory_space_constraint(x, pltpu.HBM)
            for x in (
                volume.reshape(cin * cells, depth), w, bias.reshape(1, cout), upstream.reshape(cout * cells, depth)
            )
        )
    )
    act, ig, wg, bg = pl.pallas_call(
        functools.partial(finish, norm, cin, cout),
        out_shape=(act_out, ig_out, wg_out, bg_out),
        in_specs=[whole] * 3,
        out_specs=[hbm] * 4,
        scratch_shapes=[v((owners * crows, 2 * cout), F32), v((27, cin, cout), F32), v((1, cout), F32), dma((4,))],
        compiler_params=pltpu.CompilerParams(vmem_limit_bytes=16 << 20),
    )(act, ig, gat)
    shape = (samples, -1, rows, cols, depth)
    filt = wg.reshape(3, 3, 3, cin, cout).transpose(4, 3, 0, 1, 2)
    return act.reshape(shape), ig.reshape(shape), filt, bg.reshape(cout)


def solution(mesh):
    block = P("samp", None, "sx", "sy", None)
    return jax.shard_map(
        per_device, mesh=mesh, in_specs=(block, P(), P(), block),
        out_specs=(block, block, P(), P()), check_vma=False,
    )
```

```python
import functools
import math

import jax
import jax.numpy as jnp
from jax import lax
from jax.experimental import pallas as pl
from jax.experimental.pallas import tpu as pltpu
from jax.sharding import PartitionSpec as P

MESH = pl.DeviceIdType.MESH
F32 = jnp.float32
BF16 = jnp.bfloat16
DIRS = tuple((dx, dy) for dx in (-1, 0, 1) for dy in (-1, 0, 1) if dx or dy)


def each(count, fn):
    if count <= 8:
        for k in range(1, count):
            fn(k)
    else:
        lax.fori_loop(1, count, lambda k, c: (fn(k), c)[1], 0)


def span(step, size):
    if step > 0:
        return pl.ds(size, 1), pl.ds(0, 1), pl.ds(size + 1, 1)
    if step < 0:
        return pl.ds(1, 1), pl.ds(size + 1, 1), pl.ds(0, 1)
    return pl.ds(1, size), pl.ds(1, size), pl.ds(1, size)


def taps(step):
    return {1: (2,), -1: (0,), 0: (0, 1, 2)}[step]


def places(step, size):
    return {1: (size + 1,), -1: (0,), 0: tuple(range(1, size + 1))}[step]


def kernel(
    dims, sizes, chunk, norm,
    vol_hbm, w_hbm, bias_hbm, up_hbm,
    act_ref, ig_ref, gat,
    vol_ref, w_ref, bias_ref, up_ref,
    vol_s, up_s, act_s, ig_s, pad, dpad, hout, hin, col, ys, act_c, up_c, dcol, sd, wt, wtt, wb, wbs, stage, part, r1, r2,
    ls, hs1, hr1, hs2, hr2, s1, v1, s2, v2, s3, v3,
):
    rows, cols, cin, cout, depth = dims
    n_samp, n_sx, n_sy = sizes
    owners, crows = chunk
    cells = rows * cols
    group = n_sx * n_sy
    me = lax.axis_index("samp")
    ix, iy = lax.axis_index("sx"), lax.axis_index("sy")
    gid = ix * n_sy + iy

    loads = [
        pltpu.make_async_copy(src, dst, ls.at[i])
        for i, (src, dst) in enumerate(
            ((vol_hbm, vol_ref), (w_hbm, w_ref), (bias_hbm, bias_ref), (up_hbm, up_ref))
        )
    ]
    for load in loads:
        load.start()
    barrier = pltpu.get_barrier_semaphore()

    def greet_samp(k):
        pl.semaphore_signal(barrier, inc=1, device_id={"samp": lax.rem(me + k, n_samp)}, device_id_type=MESH)

    def group_id(k):
        g = lax.rem(gid + k, group)
        return g, {"sx": lax.div(g, n_sy), "sy": lax.rem(g, n_sy)}

    def greet_group(k):
        pl.semaphore_signal(barrier, inc=1, device_id=group_id(k)[1], device_id_type=MESH)

    each(n_samp, greet_samp)
    each(group, greet_group)

    def has(dx, dy):
        ok = None
        for i, step, size in ((ix, dx, n_sx), (iy, dy, n_sy)):
            if step:
                one = (i + 1 < size) if step > 0 else (i > 0)
                ok = one if ok is None else jnp.logical_and(ok, one)
        return ok

    half = cols // 2 if cols % 4 == 0 else cols

    def halo(buf, ss, rs, d, piece=0):
        dx, dy = DIRS[d]
        sx, tx, ox = span(dx, rows)
        sy, ty, oy = span(dy, cols)
        if buf is pad and not dy and half < cols:
            sy = ty = pl.ds(half + 2, cols - half - 1) if piece else pl.ds(1, half + 1)
        sem = d + 8 * piece
        src = buf.at[sx, sy] if buf is pad else hout.at[ox, oy]
        return pltpu.make_async_remote_copy(
            src_ref=src, dst_ref=buf.at[tx, ty],
            send_sem=ss.at[sem], recv_sem=rs.at[sem],
            device_id={"sx": ix + dx, "sy": iy + dy}, device_id_type=MESH,
        )

    live = [d for d, (dx, dy) in enumerate(DIRS) if not ((dx and n_sx == 1) or (dy and n_sy == 1))]

    def halo_zero(buf):
        for d, (dx, dy) in enumerate(DIRS):
            _, tx, _ = span(dx, rows)
            _, ty, _ = span(dy, cols)

            def clear():
                v = buf[tx, ty]
                buf[tx, ty] = jnp.zeros_like(v)

            if d in live:
                pl.when(jnp.logical_not(has(-dx, -dy)))(clear)
            else:
                clear()

    late = [d for d in live if not DIRS[d][1]] if half < cols else []
    near = sorted(live, key=lambda d: (d in late, DIRS[d][1] == 0))

    def halo_send(buf, ss, rs):
        for d in near:
            pl.when(has(*DIRS[d]))(lambda: halo(buf, ss, rs, d).start())
        for d in late:
            pl.when(has(*DIRS[d]))(lambda: halo(buf, ss, rs, d, 1).start())

    def halo_recv(buf, ss, rs, which, piece=0):
        for d in which:
            dx, dy = DIRS[d]
            pl.when(has(-dx, -dy))(lambda: halo(buf, ss, rs, d, piece).wait_recv())

    def halo_sent(buf, ss, rs, which, piece=0):
        for d in which:
            pl.when(has(*DIRS[d]))(lambda: halo(buf, ss, rs, d, piece).wait_send())

    loads[0].wait()
    vol_s[...] = vol_ref[...].astype(F32)
    for x in range(rows):
        for y in range(cols):
            pad[1 + x, 1 + y] = vol_s[pl.ds(x * cols + y, cin, stride=cells), :].astype(BF16)
    pl.semaphore_wait(barrier, n_samp - 1 + group - 1)
    halo_send(pad, hs1, hr1)
    halo_zero(pad)
    halo_zero(hin)
    for x in (0, rows + 1):
        dpad[x] = jnp.zeros((cols + 2, cout, depth), BF16)
    for x in range(1, rows + 1):
        for y in (0, cols + 1):
            dpad[x, y] = jnp.zeros((cout, depth), BF16)
    for load in loads[1:]:
        load.wait()
    for g in range(9):
        for c in range(3):
            block = w_ref[g * 3 + c]
            wt[g * cin:(g + 1) * cin, c * cout:(c + 1) * cout] = block
            wb[c * cin:(c + 1) * cin, g * cout:(g + 1) * cout] = block
            wbs[g, c * cin:(c + 1) * cin, :] = block
    wtt[...] = wt[...].T
    up_s[...] = up_ref[...].astype(F32)
    for n in range(cells):
        up_c[n] = up_s[pl.ds(n, cout, stride=cells), :]
    col[9 * cin:, :] = jnp.ones((16, cells * depth), BF16)
    eye = lax.broadcasted_iota(jnp.int32, (cout, cout), 0) == lax.broadcasted_iota(jnp.int32, (cout, cout), 1)
    bias = jnp.sum(jnp.where(eye, bias_ref[...], 0.0), axis=1, keepdims=True)
    lane_i = lax.broadcasted_iota(jnp.int32, (cin, depth), 1)

    def ahead(v, lanes):
        return jnp.where(lanes < depth - 1, pltpu.roll(v, depth - 1, 1), 0.0)

    def behind(v, lanes):
        return jnp.where(lanes > 0, pltpu.roll(v, 1, 1), 0.0)

    step = 2 if cols % 2 == 0 else 1
    sub = cout // 2 if cout % 32 == 0 else cout

    def columns(lo, hi):
        for x in range(rows):
            for y in range(lo, hi):
                n = x * cols + y
                for a in range(3):
                    for b in range(3):
                        g = a * 3 + b
                        col[g * cin:(g + 1) * cin, n * depth:(n + 1) * depth] = pad[x + a, y + b]

    def product(m):
        at = slice(m * depth, (m + step) * depth)
        ys[:, at] = jnp.dot(wtt[...], col[0:9 * cin, at], preferred_element_type=F32)

    def pointwise(n, h):
        at = slice(n * depth, (n + 1) * depth)
        lane = lax.broadcasted_iota(jnp.int32, (sub, depth), 1)
        y0, y1, y2 = (ys[c * cout + h:c * cout + h + sub, at] for c in range(3))
        pre = behind(y0, lane) + y1 + ahead(y2, lane) + bias[h:h + sub]
        t = jnp.exp(-jnp.abs(pre))
        one = 1.0 + t
        soft = jnp.maximum(pre, 0.0) + jnp.log(one)
        sig = jnp.where(pre >= 0, 1.0, t) / one
        act_c[n, h:h + sub, :] = 0.3 * pre + 0.7 * soft
        d16 = (up_c[n, h:h + sub, :] * (0.3 + 0.7 * sig)).astype(BF16)
        dpad[1 + n // cols, 1 + n % cols, h:h + sub, :] = d16
        d = d16.astype(F32)
        sd[h:h + sub, at] = ahead(d, lane).astype(BF16)
        sd[cout + h:cout + h + sub, at] = d16
        sd[2 * cout + h:2 * cout + h + sub, at] = behind(d, lane).astype(BF16)

    def forward(lo, hi):
        columns(lo, hi)
        ms = [x * cols + y for x in range(rows) for y in range(lo, hi, step)]
        product(ms[0])
        for i, m in enumerate(ms):
            if i + 1 < len(ms):
                product(ms[i + 1])
            for n in range(m, m + step):
                for h in range(0, cout, sub):
                    pointwise(n, h)

    halo_recv(pad, hs1, hr1, live)
    forward(0, half)
    if half < cols:
        halo_recv(pad, hs1, hr1, late, 1)
        forward(half, cols)

    dw = lax.dot_general(col[...], sd[...], (((1,), (1,)), ((), ())), preferred_element_type=F32)
    k9, o2, five = 9 * cin, 2 * cout, 5 * cin
    stage[k9 + five - cin:, :] = jnp.zeros_like(stage[k9 + five - cin:, :])
    stage[0:k9, :] = dw[0:k9, 0:o2]
    stage[k9:k9 + five, 0:cout] = dw[0:five, o2:]
    stage[k9:k9 + k9 - five, cout:] = dw[five:k9, o2:]
    brow = k9 + k9 - five
    stage[brow:brow + 16, cout:] = dw[k9:, cout:o2]
    for q in range(owners):
        part[q] = stage[q * crows:(q + 1) * crows, :].astype(BF16)

    def when(cond, fn, always):
        if always:
            fn()
        else:
            pl.when(cond)(fn)

    every = owners == n_samp
    mine = me < owners

    def rs(src, dst, p):
        return pltpu.make_async_remote_copy(
            src_ref=part.at[src], dst_ref=r1.at[dst], send_sem=s1.at[src], recv_sem=v1.at[dst],
            device_id={"samp": p}, device_id_type=MESH,
        )

    def rs_start(k):
        p = lax.rem(me + k, n_samp)
        when(p < owners, lambda: rs(p, me, p).start(), every)

    def rs_sent(k):
        p = lax.rem(me + k, n_samp)
        when(p < owners, lambda: rs(p, me, p).wait_send(), every)

    each(n_samp, rs_start)

    def outside(d):
        dx, dy = DIRS[d]
        spots = [(x, y) for x in places(dx, rows) for y in places(dy, cols)]
        for m in range(0, len(spots), 2):
            pair = spots[m:m + 2]
            out = None
            for a in taps(dx):
                for b in taps(dy):
                    rhs = jnp.concatenate([dpad[x + 1 - a, y + 1 - b] for x, y in pair], axis=1)
                    term = jnp.dot(wbs[a * 3 + b], rhs, preferred_element_type=F32)
                    out = term if out is None else out + term
            for n, (x, y) in enumerate(pair):
                u0, u1, u2 = (out[c * cin:(c + 1) * cin, n * depth:(n + 1) * depth] for c in range(3))
                hout[x, y] = (ahead(u0, lane_i) + u1 + behind(u2, lane_i)).astype(BF16)
        halo(hin, hs2, hr2, d).start()

    for d in live:
        pl.when(has(*DIRS[d]))(lambda: outside(d))
    for x in range(rows):
        for y in range(cols):
            n = x * cols + y
            for a in range(3):
                for b in range(3):
                    g = a * 3 + b
                    dcol[g * cout:(g + 1) * cout, n * depth:(n + 1) * depth] = dpad[x + 2 - a, y + 2 - b]

    def backward(lo, hi):
        for m in range(lo, hi, step):
            out = jnp.dot(wb[...], dcol[:, m * depth:(m + step) * depth], preferred_element_type=F32)
            for n in range(m, m + step):
                k = (n - m) * depth
                u0, u1, u2 = (out[c * cin:(c + 1) * cin, k:k + depth] for c in range(3))
                ig_s[pl.ds(n, cin, stride=cells), :] = ahead(u0, lane_i) + u1 + behind(u2, lane_i)

    def gs(k):
        g, dev = group_id(k)
        return pltpu.make_async_remote_copy(
            src_ref=r2.at[gid], dst_ref=r2.at[gid], send_sem=s2.at[g], recv_sem=v2.at[gid],
            device_id=dev, device_id_type=MESH,
        )

    def gs_from(k):
        g, dev = group_id(k)
        return pltpu.make_async_remote_copy(
            src_ref=r2.at[g], dst_ref=r2.at[g], send_sem=s2.at[g], recv_sem=v2.at[g],
            device_id=dev, device_id_type=MESH,
        )

    def reduce_own():
        each(n_samp, lambda k: rs(0, lax.rem(me + k, n_samp), 0).wait_recv())
        r1[me] = part[me]
        total = lax.fori_loop(1, n_samp, lambda j, t: t + r1[j].astype(F32), r1[0].astype(F32))
        r2[gid] = total.astype(BF16)
        each(group, lambda k: gs(k).start())

    def ag(slot, p, sem):
        return pltpu.make_async_remote_copy(
            src_ref=gat.at[slot], dst_ref=gat.at[slot], send_sem=s3.at[sem], recv_sem=v3.at[slot],
            device_id={"samp": p}, device_id_type=MESH,
        )

    def ag_start(k):
        p = lax.rem(me + k, n_samp)
        ag(me, p, p).start()

    def gather_own():
        each(group, lambda k: gs_from(k).wait_recv())
        total = r2[0].astype(F32)
        for j in range(1, group):
            total = total + r2[j].astype(F32)
        gat[me] = total.astype(BF16)
        each(n_samp, ag_start)

    backward(0, cells)
    when(mine, reduce_own, every)
    halo_recv(hin, hs2, hr2, live)
    for x in range(1, rows + 1):
        for y in range(1, cols + 1):
            spots = []
            for dx in (-1, 0, 1):
                for dy in (-1, 0, 1):
                    if (dx or dy) and (not dx or x == (1 if dx < 0 else rows)) and (not dy or y == (1 if dy < 0 else cols)):
                        spots.append((x + dx, y + dy))
            if spots:
                at = pl.ds((x - 1) * cols + y - 1, cin, stride=cells)
                total = ig_s[at, :]
                for spot in spots:
                    total = total + hin[spot].astype(F32)
                ig_s[at, :] = total
    ig_ref[...] = ig_s[...].astype(BF16)
    when(mine, gather_own, every)
    for n in range(cells):
        act_s[pl.ds(n, cout, stride=cells), :] = act_c[n]
    act_ref[...] = act_s[...].astype(BF16)

    def ag_recv(k):
        p = lax.rem(me + k, n_samp)
        when(p < owners, lambda: ag(p, p, p).wait_recv(), every)

    each(n_samp, ag_recv)
    halo_sent(pad, hs1, hr1, live)
    halo_sent(pad, hs1, hr1, late, 1)
    halo_sent(hin, hs2, hr2, live)
    each(n_samp, rs_sent)

    def own_sent():
        each(group, lambda k: gs(k).wait_send())
        each(n_samp, lambda k: ag(me, lax.rem(me + k, n_samp), lax.rem(me + k, n_samp)).wait_send())

    when(mine, own_sent, every)


def finish(norm, cin, cout, act_ref, ig_ref, gat, act_hbm, ig_hbm, wg_hbm, bg_hbm, stage, wg_ref, bg_ref, sem):
    copies = [
        pltpu.make_async_copy(src, dst, sem.at[i])
        for i, (src, dst) in enumerate(
            ((act_ref, act_hbm), (ig_ref, ig_hbm), (wg_ref, wg_hbm), (bg_ref, bg_hbm))
        )
    ]
    copies[0].start()
    copies[1].start()
    owners, crows, _ = gat.shape
    k9, half = 9 * cin, 5 * cin
    for q in range(owners):
        stage[q * crows:(q + 1) * crows, :] = gat[q].astype(F32) * norm
    for g in range(9):
        lo = g * cin
        wg_ref[g * 3] = stage[lo:lo + cin, 0:cout]
        wg_ref[g * 3 + 1] = stage[lo:lo + cin, cout:]
        if g < 5:
            wg_ref[g * 3 + 2] = stage[k9 + lo:k9 + lo + cin, 0:cout]
        else:
            wg_ref[g * 3 + 2] = stage[k9 + lo - half:k9 + lo - half + cin, cout:]
    brow = k9 + k9 - half
    bg_ref[...] = stage[brow:brow + 1, cout:]
    copies[2].start()
    copies[3].start()
    for copy in copies:
        copy.wait()


def per_device(volume, kern, bias, upstream):
    samples, cin, rows, cols, depth = volume.shape
    cout = kern.shape[0]
    sizes = tuple(lax.axis_size(a) for a in ("samp", "sx", "sy"))
    cells = rows * cols
    packed = 14 * cin
    owners = min(sizes[0], 7)
    crows = -(-packed // (owners * 16)) * 16
    norm = 1.0 / math.sqrt(sizes[0] * samples * sizes[1] * sizes[2] * cells * depth)
    group = sizes[1] * sizes[2]
    dma = pltpu.SemaphoreType.DMA
    v = pltpu.VMEM
    whole = pl.BlockSpec(memory_space=pltpu.VMEM)
    w = kern.transpose(2, 3, 4, 1, 0).reshape(27, cin, cout)
    hbm = pl.BlockSpec(memory_space=pltpu.HBM)
    act_out = jax.ShapeDtypeStruct((cout * cells, depth), BF16)
    ig_out = jax.ShapeDtypeStruct((cin * cells, depth), BF16)
    wg_out = jax.ShapeDtypeStruct((27, cin, cout), F32)
    bg_out = jax.ShapeDtypeStruct((1, cout), F32)
    act, ig, gat = pl.pallas_call(
        functools.partial(kernel, (rows, cols, cin, cout, depth), sizes, (owners, crows), norm),
        out_shape=(act_out, ig_out, jax.ShapeDtypeStruct((owners, crows, 2 * cout), BF16)),
        in_specs=[hbm] * 4,
        out_specs=[whole] * 3,
        scratch_shapes=[
            v((cin * cells, depth), BF16), v((27, cin, cout), BF16), v((1, cout), F32), v((cout * cells, depth), BF16),
            v((cin * cells, depth), F32), v((cout * cells, depth), F32),
            v((cout * cells, depth), F32), v((cin * cells, depth), F32),
            v((rows + 2, cols + 2, cin, depth), BF16), v((rows + 2, cols + 2, cout, depth), BF16),
            v((rows + 2, cols + 2, cin, depth), BF16), v((rows + 2, cols + 2, cin, depth), BF16),
            v((9 * cin + 16, cells * depth), BF16), v((3 * cout, cells * depth), F32),
            v((cells, cout, depth), F32), v((cells, cout, depth), F32), v((9 * cout, cells * depth), BF16),
            v((3 * cout, cells * depth), BF16),
            v((9 * cin, 3 * cout), BF16), v((3 * cout, 9 * cin), BF16), v((3 * cin, 9 * cout), BF16),
            v((9, 3 * cin, cout), BF16),
            v((owners * crows, 2 * cout), F32), v((owners, crows, 2 * cout), BF16),
            v((sizes[0], crows, 2 * cout), BF16), v((group, crows, 2 * cout), BF16),
            dma((4,)), dma((16,)), dma((16,)), dma((8,)), dma((8,)),
            dma((owners,)), dma((sizes[0],)), dma((group,)), dma((group,)),
            dma((sizes[0],)), dma((owners,)),
        ],
        compiler_params=pltpu.CompilerParams(
            collective_id=0, has_side_effects=True, vmem_limit_bytes=40 << 20
        ),
    )(
        *(
            pltpu.with_memory_space_constraint(x, pltpu.HBM)
            for x in (
                volume.reshape(cin * cells, depth), w, bias.reshape(1, cout), upstream.reshape(cout * cells, depth)
            )
        )
    )
    act, ig, wg, bg = pl.pallas_call(
        functools.partial(finish, norm, cin, cout),
        out_shape=(act_out, ig_out, wg_out, bg_out),
        in_specs=[whole] * 3,
        out_specs=[hbm] * 4,
        scratch_shapes=[v((owners * crows, 2 * cout), F32), v((27, cin, cout), F32), v((1, cout), F32), dma((4,))],
        compiler_params=pltpu.CompilerParams(vmem_limit_bytes=16 << 20),
    )(act, ig, gat)
    shape = (samples, -1, rows, cols, depth)
    filt = wg.reshape(3, 3, 3, cin, cout).transpose(4, 3, 0, 1, 2)
    return act.reshape(shape), ig.reshape(shape), filt, bg.reshape(cout)


def solution(mesh):
    block = P("samp", None, "sx", "sy", None)
    return jax.shard_map(
        per_device, mesh=mesh, in_specs=(block, P(), P(), block),
        out_specs=(block, block, P(), P()), check_vma=False,
    )
```

```python
import functools
import math

import jax
import jax.numpy as jnp
from jax import lax
from jax.experimental import pallas as pl
from jax.experimental.pallas import tpu as pltpu
from jax.sharding import PartitionSpec as P

MESH = pl.DeviceIdType.MESH
F32 = jnp.float32
BF16 = jnp.bfloat16
DIRS = tuple((dx, dy) for dx in (-1, 0, 1) for dy in (-1, 0, 1) if dx or dy)


def each(count, fn):
    if count <= 8:
        for k in range(1, count):
            fn(k)
    else:
        lax.fori_loop(1, count, lambda k, c: (fn(k), c)[1], 0)


def span(step, size):
    if step > 0:
        return pl.ds(size, 1), pl.ds(0, 1), pl.ds(size + 1, 1)
    if step < 0:
        return pl.ds(1, 1), pl.ds(size + 1, 1), pl.ds(0, 1)
    return pl.ds(1, size), pl.ds(1, size), pl.ds(1, size)


def taps(step):
    return {1: (2,), -1: (0,), 0: (0, 1, 2)}[step]


def places(step, size):
    return {1: (size + 1,), -1: (0,), 0: tuple(range(1, size + 1))}[step]


def kernel(
    dims, sizes, chunk, norm,
    vol_hbm, w_hbm, bias_hbm, up_hbm,
    act_ref, ig_ref, gat,
    vol_ref, w_ref, bias_ref, up_ref,
    vol_s, up_s, act_s, ig_s, pad, dpad, hout, hin, col, ys, act_c, up_c, dcol, sd, wt, wtt, wb, wbs, stage, part, r1, r2,
    ls, hs1, hr1, hs2, hr2, s1, v1, s2, v2, s3, v3,
):
    rows, cols, cin, cout, depth = dims
    n_samp, n_sx, n_sy = sizes
    owners, crows = chunk
    cells = rows * cols
    group = n_sx * n_sy
    me = lax.axis_index("samp")
    ix, iy = lax.axis_index("sx"), lax.axis_index("sy")
    gid = ix * n_sy + iy

    loads = [
        pltpu.make_async_copy(src, dst, ls.at[i])
        for i, (src, dst) in enumerate(
            ((vol_hbm, vol_ref), (w_hbm, w_ref), (bias_hbm, bias_ref), (up_hbm, up_ref))
        )
    ]
    for load in loads:
        load.start()
    barrier = pltpu.get_barrier_semaphore()

    def greet_samp(k):
        pl.semaphore_signal(barrier, inc=1, device_id={"samp": lax.rem(me + k, n_samp)}, device_id_type=MESH)

    def group_id(k):
        g = lax.rem(gid + k, group)
        return g, {"sx": lax.div(g, n_sy), "sy": lax.rem(g, n_sy)}

    def greet_group(k):
        pl.semaphore_signal(barrier, inc=1, device_id=group_id(k)[1], device_id_type=MESH)

    each(n_samp, greet_samp)
    each(group, greet_group)

    def has(dx, dy):
        ok = None
        for i, step, size in ((ix, dx, n_sx), (iy, dy, n_sy)):
            if step:
                one = (i + 1 < size) if step > 0 else (i > 0)
                ok = one if ok is None else jnp.logical_and(ok, one)
        return ok

    half = cols // 2 if cols % 4 == 0 else cols

    def halo(buf, ss, rs, d, piece=0):
        dx, dy = DIRS[d]
        sx, tx, ox = span(dx, rows)
        sy, ty, oy = span(dy, cols)
        if buf is pad and not dy and half < cols:
            sy = ty = pl.ds(half + 2, cols - half - 1) if piece else pl.ds(1, half + 1)
        sem = d + 8 * piece
        src = buf.at[sx, sy] if buf is pad else hout.at[ox, oy]
        return pltpu.make_async_remote_copy(
            src_ref=src, dst_ref=buf.at[tx, ty],
            send_sem=ss.at[sem], recv_sem=rs.at[sem],
            device_id={"sx": ix + dx, "sy": iy + dy}, device_id_type=MESH,
        )

    live = [d for d, (dx, dy) in enumerate(DIRS) if not ((dx and n_sx == 1) or (dy and n_sy == 1))]

    def halo_zero(buf):
        for d, (dx, dy) in enumerate(DIRS):
            _, tx, _ = span(dx, rows)
            _, ty, _ = span(dy, cols)

            def clear():
                v = buf[tx, ty]
                buf[tx, ty] = jnp.zeros_like(v)

            if d in live:
                pl.when(jnp.logical_not(has(-dx, -dy)))(clear)
            else:
                clear()

    late = [d for d in live if not DIRS[d][1]] if half < cols else []
    near = sorted(live, key=lambda d: (d in late, DIRS[d][1] == 0))

    def halo_send(buf, ss, rs):
        for d in near:
            pl.when(has(*DIRS[d]))(lambda: halo(buf, ss, rs, d).start())
        for d in late:
            pl.when(has(*DIRS[d]))(lambda: halo(buf, ss, rs, d, 1).start())

    def halo_recv(buf, ss, rs, which, piece=0):
        for d in which:
            dx, dy = DIRS[d]
            pl.when(has(-dx, -dy))(lambda: halo(buf, ss, rs, d, piece).wait_recv())

    def halo_sent(buf, ss, rs, which, piece=0):
        for d in which:
            pl.when(has(*DIRS[d]))(lambda: halo(buf, ss, rs, d, piece).wait_send())

    loads[0].wait()
    vol_s[...] = vol_ref[...].astype(F32)
    for x in range(rows):
        for y in range(cols):
            pad[1 + x, 1 + y] = vol_s[pl.ds(x * cols + y, cin, stride=cells), :].astype(BF16)
    pl.semaphore_wait(barrier, n_samp - 1 + group - 1)
    halo_send(pad, hs1, hr1)
    halo_zero(pad)
    halo_zero(hin)
    for x in (0, rows + 1):
        dpad[x] = jnp.zeros((cols + 2, cout, depth), BF16)
    for x in range(1, rows + 1):
        for y in (0, cols + 1):
            dpad[x, y] = jnp.zeros((cout, depth), BF16)
    for load in loads[1:]:
        load.wait()
    for g in range(9):
        for c in range(3):
            block = w_ref[g * 3 + c]
            wt[g * cin:(g + 1) * cin, c * cout:(c + 1) * cout] = block
            wb[c * cin:(c + 1) * cin, g * cout:(g + 1) * cout] = block
            wbs[g, c * cin:(c + 1) * cin, :] = block
    wtt[...] = wt[...].T
    up_s[...] = up_ref[...].astype(F32)
    for n in range(cells):
        up_c[n] = up_s[pl.ds(n, cout, stride=cells), :]
    col[9 * cin:, :] = jnp.ones((16, cells * depth), BF16)
    eye = lax.broadcasted_iota(jnp.int32, (cout, cout), 0) == lax.broadcasted_iota(jnp.int32, (cout, cout), 1)
    bias = jnp.sum(jnp.where(eye, bias_ref[...], 0.0), axis=1, keepdims=True)
    lane_i = lax.broadcasted_iota(jnp.int32, (cin, depth), 1)

    def ahead(v, lanes):
        return jnp.where(lanes < depth - 1, pltpu.roll(v, depth - 1, 1), 0.0)

    def behind(v, lanes):
        return jnp.where(lanes > 0, pltpu.roll(v, 1, 1), 0.0)

    step = 2 if cols % 2 == 0 else 1
    sub = cout // 2 if cout % 32 == 0 else cout

    def columns(lo, hi):
        for x in range(rows):
            for y in range(lo, hi):
                n = x * cols + y
                for a in range(3):
                    for b in range(3):
                        g = a * 3 + b
                        col[g * cin:(g + 1) * cin, n * depth:(n + 1) * depth] = pad[x + a, y + b]

    def product(m):
        at = slice(m * depth, (m + step) * depth)
        ys[:, at] = jnp.dot(wtt[...], col[0:9 * cin, at], preferred_element_type=F32)

    def pointwise(n, h):
        at = slice(n * depth, (n + 1) * depth)
        lane = lax.broadcasted_iota(jnp.int32, (sub, depth), 1)
        y0, y1, y2 = (ys[c * cout + h:c * cout + h + sub, at] for c in range(3))
        pre = behind(y0, lane) + y1 + ahead(y2, lane) + bias[h:h + sub]
        t = jnp.exp(-jnp.abs(pre))
        one = 1.0 + t
        soft = jnp.maximum(pre, 0.0) + jnp.log(one)
        sig = jnp.where(pre >= 0, 1.0, t) / one
        act_c[n, h:h + sub, :] = 0.3 * pre + 0.7 * soft
        d16 = (up_c[n, h:h + sub, :] * (0.3 + 0.7 * sig)).astype(BF16)
        dpad[1 + n // cols, 1 + n % cols, h:h + sub, :] = d16
        d = d16.astype(F32)
        sd[h:h + sub, at] = ahead(d, lane).astype(BF16)
        sd[cout + h:cout + h + sub, at] = d16
        sd[2 * cout + h:2 * cout + h + sub, at] = behind(d, lane).astype(BF16)

    def forward(lo, hi):
        columns(lo, hi)
        ms = [x * cols + y for x in range(rows) for y in range(lo, hi, step)]
        product(ms[0])
        for i, m in enumerate(ms):
            if i + 1 < len(ms):
                product(ms[i + 1])
            for n in range(m, m + step):
                for h in range(0, cout, sub):
                    pointwise(n, h)

    halo_recv(pad, hs1, hr1, live)
    forward(0, half)
    if half < cols:
        halo_recv(pad, hs1, hr1, late, 1)
        forward(half, cols)

    dw = lax.dot_general(col[...], sd[...], (((1,), (1,)), ((), ())), preferred_element_type=F32)
    k9, o2, five = 9 * cin, 2 * cout, 5 * cin
    stage[k9 + five - cin:, :] = jnp.zeros_like(stage[k9 + five - cin:, :])
    stage[0:k9, :] = dw[0:k9, 0:o2]
    stage[k9:k9 + five, 0:cout] = dw[0:five, o2:]
    stage[k9:k9 + k9 - five, cout:] = dw[five:k9, o2:]
    brow = k9 + k9 - five
    stage[brow:brow + 16, cout:] = dw[k9:, cout:o2]
    for q in range(owners):
        part[q] = stage[q * crows:(q + 1) * crows, :].astype(BF16)

    def when(cond, fn, always):
        if always:
            fn()
        else:
            pl.when(cond)(fn)

    every = owners == n_samp
    mine = me < owners

    def rs(src, dst, p):
        return pltpu.make_async_remote_copy(
            src_ref=part.at[src], dst_ref=r1.at[dst], send_sem=s1.at[src], recv_sem=v1.at[dst],
            device_id={"samp": p}, device_id_type=MESH,
        )

    def rs_start(k):
        p = lax.rem(me + k, n_samp)
        when(p < owners, lambda: rs(p, me, p).start(), every)

    def rs_sent(k):
        p = lax.rem(me + k, n_samp)
        when(p < owners, lambda: rs(p, me, p).wait_send(), every)

    each(n_samp, rs_start)

    def outside(d):
        dx, dy = DIRS[d]
        spots = [(x, y) for x in places(dx, rows) for y in places(dy, cols)]
        for m in range(0, len(spots), 2):
            pair = spots[m:m + 2]
            out = None
            for a in taps(dx):
                for b in taps(dy):
                    rhs = jnp.concatenate([dpad[x + 1 - a, y + 1 - b] for x, y in pair], axis=1)
                    term = jnp.dot(wbs[a * 3 + b], rhs, preferred_element_type=F32)
                    out = term if out is None else out + term
            for n, (x, y) in enumerate(pair):
                u0, u1, u2 = (out[c * cin:(c + 1) * cin, n * depth:(n + 1) * depth] for c in range(3))
                hout[x, y] = (ahead(u0, lane_i) + u1 + behind(u2, lane_i)).astype(BF16)

    for d in live:
        pl.when(has(*DIRS[d]))(lambda: outside(d))
    for x in range(rows):
        for y in range(cols):
            n = x * cols + y
            for a in range(3):
                for b in range(3):
                    g = a * 3 + b
                    dcol[g * cout:(g + 1) * cout, n * depth:(n + 1) * depth] = dpad[x + 2 - a, y + 2 - b]

    def backward(lo, hi):
        for m in range(lo, hi, step):
            out = jnp.dot(wb[...], dcol[:, m * depth:(m + step) * depth], preferred_element_type=F32)
            for n in range(m, m + step):
                k = (n - m) * depth
                u0, u1, u2 = (out[c * cin:(c + 1) * cin, k:k + depth] for c in range(3))
                ig_s[pl.ds(n, cin, stride=cells), :] = ahead(u0, lane_i) + u1 + behind(u2, lane_i)

    def gs(k):
        g, dev = group_id(k)
        return pltpu.make_async_remote_copy(
            src_ref=r2.at[gid], dst_ref=r2.at[gid], send_sem=s2.at[g], recv_sem=v2.at[gid],
            device_id=dev, device_id_type=MESH,
        )

    def gs_from(k):
        g, dev = group_id(k)
        return pltpu.make_async_remote_copy(
            src_ref=r2.at[g], dst_ref=r2.at[g], send_sem=s2.at[g], recv_sem=v2.at[g],
            device_id=dev, device_id_type=MESH,
        )

    def reduce_own():
        each(n_samp, lambda k: rs(0, lax.rem(me + k, n_samp), 0).wait_recv())
        r1[me] = part[me]
        total = lax.fori_loop(1, n_samp, lambda j, t: t + r1[j].astype(F32), r1[0].astype(F32))
        r2[gid] = total.astype(BF16)
        each(group, lambda k: gs(k).start())

    def ag(slot, p, sem):
        return pltpu.make_async_remote_copy(
            src_ref=gat.at[slot], dst_ref=gat.at[slot], send_sem=s3.at[sem], recv_sem=v3.at[slot],
            device_id={"samp": p}, device_id_type=MESH,
        )

    def ag_start(k):
        p = lax.rem(me + k, n_samp)
        ag(me, p, p).start()

    def gather_own():
        each(group, lambda k: gs_from(k).wait_recv())
        total = r2[0].astype(F32)
        for j in range(1, group):
            total = total + r2[j].astype(F32)
        gat[me] = total.astype(BF16)
        each(n_samp, ag_start)

    backward(0, cells)
    when(mine, reduce_own, every)
    for d in live:
        pl.when(has(*DIRS[d]))(lambda: halo(hin, hs2, hr2, d).start())
    when(mine, gather_own, every)
    for n in range(cells):
        act_s[pl.ds(n, cout, stride=cells), :] = act_c[n]
    act_ref[...] = act_s[...].astype(BF16)
    halo_recv(hin, hs2, hr2, live)
    for x in range(1, rows + 1):
        for y in range(1, cols + 1):
            spots = []
            for dx in (-1, 0, 1):
                for dy in (-1, 0, 1):
                    if (dx or dy) and (not dx or x == (1 if dx < 0 else rows)) and (not dy or y == (1 if dy < 0 else cols)):
                        spots.append((x + dx, y + dy))
            if spots:
                at = pl.ds((x - 1) * cols + y - 1, cin, stride=cells)
                total = ig_s[at, :]
                for spot in spots:
                    total = total + hin[spot].astype(F32)
                ig_s[at, :] = total
    ig_ref[...] = ig_s[...].astype(BF16)

    def ag_recv(k):
        p = lax.rem(me + k, n_samp)
        when(p < owners, lambda: ag(p, p, p).wait_recv(), every)

    each(n_samp, ag_recv)
    halo_sent(pad, hs1, hr1, live)
    halo_sent(pad, hs1, hr1, late, 1)
    halo_sent(hin, hs2, hr2, live)
    each(n_samp, rs_sent)

    def own_sent():
        each(group, lambda k: gs(k).wait_send())
        each(n_samp, lambda k: ag(me, lax.rem(me + k, n_samp), lax.rem(me + k, n_samp)).wait_send())

    when(mine, own_sent, every)


def finish(norm, cin, cout, act_ref, ig_ref, gat, act_hbm, ig_hbm, wg_hbm, bg_hbm, stage, wg_ref, bg_ref, sem):
    copies = [
        pltpu.make_async_copy(src, dst, sem.at[i])
        for i, (src, dst) in enumerate(
            ((act_ref, act_hbm), (ig_ref, ig_hbm), (wg_ref, wg_hbm), (bg_ref, bg_hbm))
        )
    ]
    copies[0].start()
    copies[1].start()
    owners, crows, _ = gat.shape
    k9, half = 9 * cin, 5 * cin
    for q in range(owners):
        stage[q * crows:(q + 1) * crows, :] = gat[q].astype(F32) * norm
    for g in range(9):
        lo = g * cin
        wg_ref[g * 3] = stage[lo:lo + cin, 0:cout]
        wg_ref[g * 3 + 1] = stage[lo:lo + cin, cout:]
        if g < 5:
            wg_ref[g * 3 + 2] = stage[k9 + lo:k9 + lo + cin, 0:cout]
        else:
            wg_ref[g * 3 + 2] = stage[k9 + lo - half:k9 + lo - half + cin, cout:]
    brow = k9 + k9 - half
    bg_ref[...] = stage[brow:brow + 1, cout:]
    copies[2].start()
    copies[3].start()
    for copy in copies:
        copy.wait()


def per_device(volume, kern, bias, upstream):
    samples, cin, rows, cols, depth = volume.shape
    cout = kern.shape[0]
    sizes = tuple(lax.axis_size(a) for a in ("samp", "sx", "sy"))
    cells = rows * cols
    packed = 14 * cin
    owners = min(sizes[0], 7)
    crows = -(-packed // (owners * 16)) * 16
    norm = 1.0 / math.sqrt(sizes[0] * samples * sizes[1] * sizes[2] * cells * depth)
    group = sizes[1] * sizes[2]
    dma = pltpu.SemaphoreType.DMA
    v = pltpu.VMEM
    whole = pl.BlockSpec(memory_space=pltpu.VMEM)
    w = kern.transpose(2, 3, 4, 1, 0).reshape(27, cin, cout)
    hbm = pl.BlockSpec(memory_space=pltpu.HBM)
    act_out = jax.ShapeDtypeStruct((cout * cells, depth), BF16)
    ig_out = jax.ShapeDtypeStruct((cin * cells, depth), BF16)
    wg_out = jax.ShapeDtypeStruct((27, cin, cout), F32)
    bg_out = jax.ShapeDtypeStruct((1, cout), F32)
    act, ig, gat = pl.pallas_call(
        functools.partial(kernel, (rows, cols, cin, cout, depth), sizes, (owners, crows), norm),
        out_shape=(act_out, ig_out, jax.ShapeDtypeStruct((owners, crows, 2 * cout), BF16)),
        in_specs=[hbm] * 4,
        out_specs=[whole] * 3,
        scratch_shapes=[
            v((cin * cells, depth), BF16), v((27, cin, cout), BF16), v((1, cout), F32), v((cout * cells, depth), BF16),
            v((cin * cells, depth), F32), v((cout * cells, depth), F32),
            v((cout * cells, depth), F32), v((cin * cells, depth), F32),
            v((rows + 2, cols + 2, cin, depth), BF16), v((rows + 2, cols + 2, cout, depth), BF16),
            v((rows + 2, cols + 2, cin, depth), BF16), v((rows + 2, cols + 2, cin, depth), BF16),
            v((9 * cin + 16, cells * depth), BF16), v((3 * cout, cells * depth), F32),
            v((cells, cout, depth), F32), v((cells, cout, depth), F32), v((9 * cout, cells * depth), BF16),
            v((3 * cout, cells * depth), BF16),
            v((9 * cin, 3 * cout), BF16), v((3 * cout, 9 * cin), BF16), v((3 * cin, 9 * cout), BF16),
            v((9, 3 * cin, cout), BF16),
            v((owners * crows, 2 * cout), F32), v((owners, crows, 2 * cout), BF16),
            v((sizes[0], crows, 2 * cout), BF16), v((group, crows, 2 * cout), BF16),
            dma((4,)), dma((16,)), dma((16,)), dma((8,)), dma((8,)),
            dma((owners,)), dma((sizes[0],)), dma((group,)), dma((group,)),
            dma((sizes[0],)), dma((owners,)),
        ],
        compiler_params=pltpu.CompilerParams(
            collective_id=0, has_side_effects=True, vmem_limit_bytes=40 << 20
        ),
    )(
        *(
            pltpu.with_memory_space_constraint(x, pltpu.HBM)
            for x in (
                volume.reshape(cin * cells, depth), w, bias.reshape(1, cout), upstream.reshape(cout * cells, depth)
            )
        )
    )
    act, ig, wg, bg = pl.pallas_call(
        functools.partial(finish, norm, cin, cout),
        out_shape=(act_out, ig_out, wg_out, bg_out),
        in_specs=[whole] * 3,
        out_specs=[hbm] * 4,
        scratch_shapes=[v((owners * crows, 2 * cout), F32), v((27, cin, cout), F32), v((1, cout), F32), dma((4,))],
        compiler_params=pltpu.CompilerParams(vmem_limit_bytes=16 << 20),
    )(act, ig, gat)
    shape = (samples, -1, rows, cols, depth)
    filt = wg.reshape(3, 3, 3, cin, cout).transpose(4, 3, 0, 1, 2)
    return act.reshape(shape), ig.reshape(shape), filt, bg.reshape(cout)


def solution(mesh):
    block = P("samp", None, "sx", "sy", None)
    return jax.shard_map(
        per_device, mesh=mesh, in_specs=(block, P(), P(), block),
        out_specs=(block, block, P(), P()), check_vma=False,
    )
```
